32 devices in a mesh: groups: 2 (over x), seq: 16 (over z, y, core).
Axes of the slice: x: 2, y: 2, z: 4, core: 2. Of those that a mesh axis runs over, the one named last changes fastest.
Arguments:
- queries: bfloat16 [4096, 2048], P(('groups', 'seq')), parts along dimension 0, may hold values from -6 to 6
- keys: bfloat16 [4096, 2048], P(('groups', 'seq')), parts along dimension 0, may hold values from -6 to 6
- values: bfloat16 [4096, 2048], P(('groups', 'seq')), parts along dimension 0, may hold values from -6 to 6
- gain_q: float32 [128], replicated, may hold values from 0.5 to 1.5
- gain_k: float32 [128], replicated, may hold values from 0.5 to 1.5
- w_latent: bfloat16 [2048, 512], replicated, may hold values from -0.125 to 0.125
- w_temporal: bfloat16 [3, 512, 512], replicated, may hold values from -0.15625 to 0.15625
- w_decode: bfloat16 [512, 512], replicated, may hold values from -0.25 to 0.25
Outputs:
- attention: bfloat16 [4096, 2048], P(('groups', 'seq')), parts along dimension 0
- decoded: bfloat16 [4096, 512], P(('groups', 'seq')), parts along dimension 0
The draws below stay inside these ranges and needn't reach their ends.
There are 2 independent parts, one for each index of `groups`. The reference program is written for one: setup_inputs(seed, part) draws one part's arguments, and reference() takes and returns one part's arrays. A program takes and returns all parts, laid end to end along the dimension named above; an argument that names none is the same for every part. Nothing has to cross between parts.
All inputs are finite; a program needn't handle non-finite values.
Results may differ from the reference program's by a relative error of at most 0.012.
The reference program's roundings to bfloat16 on the way count: a program that leaves them out, or rounds other values in their place, can miss the bound.
Values may be sent and summed in bfloat16 or wider, within the bound.
No kernel may reach another device: no remote copies, remote signals or barrier semaphores. Data moves between devices by JAX's collectives and lax.ppermute only.
A program may use at most 128 MiB of HBM per device.

```python
import math
import jax
import jax.numpy as jnp
from jax import lax

HEADS = 16
HD = 128
CH = 512
TAPS = 3
SPATIAL = 128
TOKENS = 2048
HH = 2048


def levels(key, extent, pieces, smallest, largest):
    level, own = 1.0, jax.random.fold_in(key, 6)
    for position, blocks in pieces:
        heights = jnp.exp(jax.random.uniform(jax.random.fold_in(own, position), (blocks,), jnp.float32, smallest / len(pieces), largest / len(pieces)))
        level = level * jnp.repeat(heights, extent[position] // blocks).reshape([-1 if axis == position else 1 for axis in range(len(extent))])
    return level


def noise(own_key, dims, deviation, most, cuts=(), held_as=jnp.bfloat16):
    result = jax.random.normal(own_key, dims, jnp.float32) * deviation
    if len(cuts) > 0:
        result = levels(own_key, dims, cuts, -0.22, 0.18) * result
    return jnp.clip(result, min=-most, max=most).astype(held_as)


def setup_inputs(seed: int = 0, part: int = 0) -> dict:
    splits = jax.random.split(jax.random.key(seed), 9)
    part_keys = jax.random.split(jax.random.fold_in(splits[8], part), 9)
    queries = noise(part_keys[0], (TOKENS, HH), 1.0, 6.0, ((0, 16),))
    keys = noise(part_keys[1], (TOKENS, HH), 1.0, 6.0, ((0, 16),))
    values = noise(part_keys[2], (TOKENS, HH), 1.0, 6.0, ((0, 16),))
    gain_q = jnp.clip(1.0 + 0.1 * jax.random.normal(splits[3], (HD,), jnp.float32), 0.5, 1.5)
    gain_k = jnp.clip(1.0 + 0.1 * jax.random.normal(splits[4], (HD,), jnp.float32), 0.5, 1.5)
    w_latent = noise(splits[5], (HH, CH), HH ** -0.5, 0.125)
    w_temporal = noise(splits[6], (TAPS, CH, CH), (TAPS * CH) ** -0.5, 0.15625)
    w_decode = noise(splits[7], (CH, CH), CH ** -0.5, 0.25)
    return {"queries": queries, "keys": keys, "values": values, "gain_q": gain_q, "gain_k": gain_k, "w_latent": w_latent, "w_temporal": w_temporal, "w_decode": w_decode}


def head_norm(x, gain):
    x = x.astype(jnp.float32).reshape(x.shape[0], HEADS, HD)
    x = x * lax.rsqrt(lax.optimization_barrier(jnp.mean(x * x, axis=-1, keepdims=True)) + 1e-06) * gain
    return x.astype(jnp.bfloat16)

def reference(queries, keys, values, gain_q, gain_k, w_latent, w_temporal, w_decode):
    qn = jnp.transpose(head_norm(queries, gain_q), (1, 0, 2))
    kn = jnp.transpose(head_norm(keys, gain_k), (1, 0, 2))
    vh = jnp.transpose(values.reshape(TOKENS, HEADS, HD), (1, 0, 2))
    block = math.gcd(TOKENS, 1024)
    scale = 1.0 / math.sqrt(HD)

    def one_head(args):
        qh, kh, vv = args

        def one_block(qb):
            scores = jnp.dot(qb, kh.T, preferred_element_type=jnp.float32) * scale
            top = lax.optimization_barrier(jnp.max(scores, axis=-1, keepdims=True))
            expo = jnp.exp(scores - top)
            total = lax.optimization_barrier(jnp.sum(expo, axis=-1, keepdims=True))
            out = jnp.dot(expo.astype(jnp.bfloat16), vv, preferred_element_type=jnp.float32)
            return (out / total).astype(jnp.bfloat16)
        outs = lax.map(one_block, qh.reshape(TOKENS // block, block, HD))
        return outs.reshape(TOKENS, HD)
    heads_out = lax.map(one_head, (qn, kn, vh))
    attention = jnp.transpose(heads_out, (1, 0, 2)).reshape(TOKENS, HH)
    latent = jnp.dot(attention, w_latent, preferred_element_type=jnp.float32).astype(jnp.bfloat16)
    zeros_row = jnp.zeros((SPATIAL, CH), jnp.bfloat16)
    earlier_one = jnp.concatenate([zeros_row, latent[:TOKENS - SPATIAL]], axis=0)
    earlier_two = jnp.concatenate([zeros_row, zeros_row, latent[:TOKENS - 2 * SPATIAL]], axis=0)
    state = jnp.dot(latent, w_temporal[0], preferred_element_type=jnp.float32)
    state = state + jnp.dot(earlier_one, w_temporal[1], preferred_element_type=jnp.float32)
    state = state + jnp.dot(earlier_two, w_temporal[2], preferred_element_type=jnp.float32)
    decoded = jnp.dot(jax.nn.silu(state).astype(jnp.bfloat16), w_decode, preferred_element_type=jnp.float32)
    return (attention, decoded.astype(jnp.bfloat16))
```

```python
import math

import jax
import jax.numpy as jnp
from jax import lax
from jax.experimental import pallas as pl
from jax.experimental.pallas import tpu as pltpu
from jax.sharding import PartitionSpec as P

HEADS = 16
HD = 128
EPS = 1e-06


def passed_along(shard, axis, by):
    peers = lax.axis_size(axis)
    pairs = [(i, i + by) for i in range(peers) if 0 <= i + by < peers]
    return lax.ppermute(shard, axis, pairs)


def _norm(x, gain):
    x = x.astype(jnp.float32)
    x = x * lax.rsqrt(jnp.mean(x * x, axis=-1, keepdims=True) + EPS) * gain
    return x.astype(jnp.bfloat16)


def _attn_kernel(share_ref, q_ref, k_ref, v_ref, gq_ref, gk_ref, o_ref, kn_ref):
    @pl.when(pl.program_id(0) == 0)
    def _():
        k = k_ref[...]
        k = k.reshape(k.shape[0] * k.shape[1], HD)
        kn_ref[...] = _norm(k, gk_ref[...])

    q = q_ref[...]
    q = q.reshape(q.shape[0] * q.shape[1], HD)
    qn = _norm(q, gq_ref[...])
    kn = kn_ref[...]
    v = v_ref[...]
    v = v.reshape(v.shape[0] * v.shape[1], HD)
    s = lax.dot_general(qn, kn, (((1,), (1,)), ((), ())), preferred_element_type=jnp.float32)
    s = s * (1.0 / math.sqrt(HD))
    m = jnp.max(s, axis=-1, keepdims=True)
    e = jnp.exp(s - m)
    total = jnp.sum(e, axis=-1, keepdims=True)
    out = jnp.dot(e.astype(jnp.bfloat16), v, preferred_element_type=jnp.float32)
    out = (out / total).astype(jnp.bfloat16)
    o_ref[...] = out.reshape(o_ref.shape)


def attend(got, share, span_blocks, gain_q, gain_k):
    src, _, rows, _ = got.shape
    qb = max(1, 512 // rows)
    qb = min(qb, span_blocks)
    steps = span_blocks // qb
    tokens = src * rows
    return pl.pallas_call(
        _attn_kernel,
        out_shape=jax.ShapeDtypeStruct((span_blocks, rows, HD), jnp.bfloat16),
        grid_spec=pltpu.PrefetchScalarGridSpec(
            num_scalar_prefetch=1,
            grid=(steps,),
            in_specs=[
                pl.BlockSpec((qb, None, rows, HD), lambda i, sh: (sh[0] * steps + i, 0, 0, 0)),
                pl.BlockSpec((src, None, rows, HD), lambda i, sh: (0, 1, 0, 0)),
                pl.BlockSpec((src, None, rows, HD), lambda i, sh: (0, 2, 0, 0)),
                pl.BlockSpec((1, HD), lambda i, sh: (0, 0)),
                pl.BlockSpec((1, HD), lambda i, sh: (0, 0)),
            ],
            out_specs=pl.BlockSpec((qb, rows, HD), lambda i, sh: (i, 0, 0)),
            scratch_shapes=[pltpu.VMEM((tokens, HD), jnp.bfloat16)],
        ),
        compiler_params=pltpu.CompilerParams(
            dimension_semantics=("arbitrary",), vmem_limit_bytes=48 * 1024 * 1024
        ),
    )(share, got, got, got, gain_q.reshape(1, HD), gain_k.reshape(1, HD))


def body(queries, keys, values, gain_q, gain_k, w_latent, w_temporal, w_decode):
    devices = lax.axis_size("seq")
    copies = devices // HEADS
    rows = queries.shape[0]

    def head_major(x):
        x = jnp.transpose(x.reshape(rows, HEADS, HD), (1, 0, 2))
        if copies > 1:
            x = jnp.broadcast_to(x[:, None], (HEADS, copies, rows, HD))
        return x.reshape(devices, rows, HD)

    stacked = jnp.stack([head_major(queries), head_major(keys), head_major(values)], axis=1)
    got = lax.all_to_all(stacked, "seq", split_axis=0, concat_axis=0, tiled=True)
    share = lax.axis_index("seq") % copies
    span_blocks = devices // copies
    out = attend(got, jnp.reshape(share, (1,)).astype(jnp.int32), span_blocks, gain_q, gain_k)
    if copies > 1:
        placed = jnp.zeros((copies, span_blocks, rows, HD), jnp.bfloat16)
        placed = lax.dynamic_update_index_in_dim(placed, out, share, 0)
        out = placed.reshape(devices, rows, HD)
    back = lax.all_to_all(out, "seq", split_axis=0, concat_axis=0, tiled=True)
    if copies > 1:
        back = jnp.sum(back.reshape(HEADS, copies, rows, HD).astype(jnp.float32), axis=1)
        back = back.astype(jnp.bfloat16)
    attention = jnp.transpose(back.reshape(HEADS, rows, HD), (1, 0, 2)).reshape(rows, HEADS * HD)
    latent = jnp.dot(attention, w_latent, preferred_element_type=jnp.float32).astype(jnp.bfloat16)
    earlier_one = passed_along(latent, "seq", 1)
    earlier_two = passed_along(latent, "seq", 2)
    state = jnp.dot(latent, w_temporal[0], preferred_element_type=jnp.float32)
    state = state + jnp.dot(earlier_one, w_temporal[1], preferred_element_type=jnp.float32)
    state = state + jnp.dot(earlier_two, w_temporal[2], preferred_element_type=jnp.float32)
    decoded = jnp.dot(
        jax.nn.silu(state).astype(jnp.bfloat16), w_decode, preferred_element_type=jnp.float32
    )
    return (attention, decoded.astype(jnp.bfloat16))


def solution(mesh):
    in_specs = (
        P(("groups", "seq"), None),
        P(("groups", "seq"), None),
        P(("groups", "seq"), None),
        P(),
        P(),
        P(),
        P(),
        P(),
    )
    out_specs = (P(("groups", "seq"), None), P(("groups", "seq"), None))
    return jax.shard_map(body, mesh=mesh, in_specs=in_specs, out_specs=out_specs, check_vma=False)
```

```python
import math

import jax
import jax.numpy as jnp
from jax import lax
from jax.experimental import pallas as pl
from jax.experimental.pallas import tpu as pltpu
from jax.sharding import PartitionSpec as P

HEADS = 16
HD = 128
EPS = 1e-06


def passed_along(shard, axis, by):
    peers = lax.axis_size(axis)
    pairs = [(i, i + by) for i in range(peers) if 0 <= i + by < peers]
    return lax.ppermute(shard, axis, pairs)


def _norm(x, gain):
    x = x.astype(jnp.float32)
    x = x * lax.rsqrt(jnp.mean(x * x, axis=-1, keepdims=True) + EPS) * gain
    return x.astype(jnp.bfloat16)


def _attn_kernel(share_ref, q_ref, k_ref, v_ref, gq_ref, gk_ref, o_ref, kn_ref):
    @pl.when(pl.program_id(0) == 0)
    def _():
        k = k_ref[...]
        k = k.reshape(k.shape[0] * k.shape[1], HD)
        kn_ref[...] = _norm(k, gk_ref[...])

    q = q_ref[...]
    q = q.reshape(q.shape[0] * q.shape[1], HD)
    qn = _norm(q, gq_ref[...])
    kn = kn_ref[...]
    v = v_ref[...]
    v = v.reshape(v.shape[0] * v.shape[1], HD)
    s = lax.dot_general(qn, kn, (((1,), (1,)), ((), ())), preferred_element_type=jnp.float32)
    s = s * (1.0 / math.sqrt(HD))
    m = jnp.max(s, axis=-1, keepdims=True)
    e = jnp.exp(s - m)
    total = jnp.sum(e, axis=-1, keepdims=True)
    out = jnp.dot(e.astype(jnp.bfloat16), v, preferred_element_type=jnp.float32)
    out = (out / total).astype(jnp.bfloat16)
    o_ref[...] = out.reshape(o_ref.shape)


def attend(got, share, span_blocks, gain_q, gain_k):
    src, _, rows, _ = got.shape
    qb = max(1, 512 // rows)
    qb = min(qb, span_blocks)
    steps = span_blocks // qb
    tokens = src * rows
    return pl.pallas_call(
        _attn_kernel,
        out_shape=jax.ShapeDtypeStruct((span_blocks, rows, HD), jnp.bfloat16),
        grid_spec=pltpu.PrefetchScalarGridSpec(
            num_scalar_prefetch=1,
            grid=(steps,),
            in_specs=[
                pl.BlockSpec((qb, None, rows, HD), lambda i, sh: (sh[0] * steps + i, 0, 0, 0)),
                pl.BlockSpec((src, None, rows, HD), lambda i, sh: (0, 1, 0, 0)),
                pl.BlockSpec((src, None, rows, HD), lambda i, sh: (0, 2, 0, 0)),
                pl.BlockSpec((1, HD), lambda i, sh: (0, 0)),
                pl.BlockSpec((1, HD), lambda i, sh: (0, 0)),
            ],
            out_specs=pl.BlockSpec((qb, rows, HD), lambda i, sh: (i, 0, 0)),
            scratch_shapes=[pltpu.VMEM((tokens, HD), jnp.bfloat16)],
        ),
        compiler_params=pltpu.CompilerParams(
            dimension_semantics=("arbitrary",), vmem_limit_bytes=48 * 1024 * 1024
        ),
    )(share, got, got, got, gain_q.reshape(1, HD), gain_k.reshape(1, HD))


def _pack_kernel(q_ref, k_ref, v_ref, o_ref):
    group = q_ref.shape[1] // HD
    copies = o_ref.shape[0] // group
    for i in range(group):
        for c in range(copies):
            for j, ref in enumerate((q_ref, k_ref, v_ref)):
                o_ref[i * copies + c, j] = ref[:, i * HD:(i + 1) * HD]


def pack(queries, keys, values, copies):
    rows = queries.shape[0]
    group = 4
    spec = pl.BlockSpec((rows, group * HD), lambda g: (0, g))
    return pl.pallas_call(
        _pack_kernel,
        out_shape=jax.ShapeDtypeStruct((HEADS * copies, 3, rows, HD), jnp.bfloat16),
        grid=(HEADS // group,),
        in_specs=[spec, spec, spec],
        out_specs=pl.BlockSpec((group * copies, 3, rows, HD), lambda g: (g, 0, 0, 0)),
    )(queries, keys, values)


def body(queries, keys, values, gain_q, gain_k, w_latent, w_temporal, w_decode):
    devices = lax.axis_size("seq")
    copies = devices // HEADS
    rows = queries.shape[0]

    stacked = pack(queries, keys, values, copies)
    got = lax.all_to_all(stacked, "seq", split_axis=0, concat_axis=0, tiled=True)
    share = lax.axis_index("seq") % copies
    span_blocks = devices // copies
    out = attend(got, jnp.reshape(share, (1,)).astype(jnp.int32), span_blocks, gain_q, gain_k)
    if copies > 1:
        placed = jnp.zeros((copies, span_blocks, rows, HD), jnp.bfloat16)
        placed = lax.dynamic_update_index_in_dim(placed, out, share, 0)
        out = placed.reshape(devices, rows, HD)
    back = lax.all_to_all(out, "seq", split_axis=0, concat_axis=0, tiled=True)
    if copies > 1:
        back = jnp.sum(back.reshape(HEADS, copies, rows, HD).astype(jnp.float32), axis=1)
        back = back.astype(jnp.bfloat16)
    attention = jnp.transpose(back.reshape(HEADS, rows, HD), (1, 0, 2)).reshape(rows, HEADS * HD)
    latent = jnp.dot(attention, w_latent, preferred_element_type=jnp.float32).astype(jnp.bfloat16)
    earlier_one = passed_along(latent, "seq", 1)
    earlier_two = passed_along(latent, "seq", 2)
    state = jnp.dot(latent, w_temporal[0], preferred_element_type=jnp.float32)
    state = state + jnp.dot(earlier_one, w_temporal[1], preferred_element_type=jnp.float32)
    state = state + jnp.dot(earlier_two, w_temporal[2], preferred_element_type=jnp.float32)
    decoded = jnp.dot(
        jax.nn.silu(state).astype(jnp.bfloat16), w_decode, preferred_element_type=jnp.float32
    )
    return (attention, decoded.astype(jnp.bfloat16))


def solution(mesh):
    in_specs = (
        P(("groups", "seq"), None),
        P(("groups", "seq"), None),
        P(("groups", "seq"), None),
        P(),
        P(),
        P(),
        P(),
        P(),
    )
    out_specs = (P(("groups", "seq"), None), P(("groups", "seq"), None))
    return jax.shard_map(body, mesh=mesh, in_specs=in_specs, out_specs=out_specs, check_vma=False)
```

```python
import math

import jax
import jax.numpy as jnp
from jax import lax
from jax.experimental import pallas as pl
from jax.experimental.pallas import tpu as pltpu
from jax.sharding import PartitionSpec as P

HEADS = 16
HD = 128
EPS = 1e-06


def passed_along(shard, axis, by):
    peers = lax.axis_size(axis)
    pairs = [(i, i + by) for i in range(peers) if 0 <= i + by < peers]
    return lax.ppermute(shard, axis, pairs)


def _norm(x, gain):
    x = x.astype(jnp.float32)
    x = x * lax.rsqrt(jnp.mean(x * x, axis=-1, keepdims=True) + EPS) * gain
    return x.astype(jnp.bfloat16)


def _attn_kernel(share_ref, q_ref, k_ref, v_ref, gq_ref, gk_ref, o_ref, kn_ref):
    @pl.when(pl.program_id(0) == 0)
    def _():
        k = k_ref[...]
        k = k.reshape(k.shape[0] * k.shape[1], HD)
        kn_ref[...] = _norm(k, gk_ref[...])

    q = q_ref[...]
    q = q.reshape(q.shape[0] * q.shape[1], HD)
    qn = _norm(q, gq_ref[...])
    kn = kn_ref[...]
    v = v_ref[...]
    v = v.reshape(v.shape[0] * v.shape[1], HD)
    s = lax.dot_general(qn, kn, (((1,), (1,)), ((), ())), preferred_element_type=jnp.float32)
    s = s * (1.0 / math.sqrt(HD))
    m = jnp.max(s, axis=-1, keepdims=True)
    e = jnp.exp(s - m)
    total = jnp.sum(e, axis=-1, keepdims=True)
    out = jnp.dot(e.astype(jnp.bfloat16), v, preferred_element_type=jnp.float32)
    out = (out / total).astype(jnp.bfloat16)
    o_ref[...] = out.reshape(o_ref.shape)


def attend(got, share, span_blocks, gain_q, gain_k, qb_rows=256):
    src, _, rows, _ = got.shape
    qb = max(1, qb_rows // rows)
    qb = min(qb, span_blocks)
    steps = span_blocks // qb
    tokens = src * rows
    return pl.pallas_call(
        _attn_kernel,
        out_shape=jax.ShapeDtypeStruct((span_blocks, rows, HD), jnp.bfloat16),
        grid_spec=pltpu.PrefetchScalarGridSpec(
            num_scalar_prefetch=1,
            grid=(steps,),
            in_specs=[
                pl.BlockSpec((qb, None, rows, HD), lambda i, sh: (sh[0] * steps + i, 0, 0, 0)),
                pl.BlockSpec((src, None, rows, HD), lambda i, sh: (0, 1, 0, 0)),
                pl.BlockSpec((src, None, rows, HD), lambda i, sh: (0, 2, 0, 0)),
                pl.BlockSpec((1, HD), lambda i, sh: (0, 0)),
                pl.BlockSpec((1, HD), lambda i, sh: (0, 0)),
            ],
            out_specs=pl.BlockSpec((qb, rows, HD), lambda i, sh: (i, 0, 0)),
            scratch_shapes=[pltpu.VMEM((tokens, HD), jnp.bfloat16)],
        ),
        compiler_params=pltpu.CompilerParams(
            dimension_semantics=("arbitrary",), vmem_limit_bytes=48 * 1024 * 1024
        ),
    )(share, got, got, got, gain_q.reshape(1, HD), gain_k.reshape(1, HD))


def _pack_kernel(q_ref, k_ref, v_ref, o_ref):
    group = q_ref.shape[1] // HD
    copies = o_ref.shape[0] // group
    for i in range(group):
        for c in range(copies):
            for j, ref in enumerate((q_ref, k_ref, v_ref)):
                o_ref[i * copies + c, j] = ref[:, i * HD:(i + 1) * HD]


def pack(queries, keys, values, copies):
    rows = queries.shape[0]
    group = 8
    spec = pl.BlockSpec((rows, group * HD), lambda g: (0, g))
    return pl.pallas_call(
        _pack_kernel,
        out_shape=jax.ShapeDtypeStruct((HEADS * copies, 3, rows, HD), jnp.bfloat16),
        grid=(HEADS // group,),
        in_specs=[spec, spec, spec],
        out_specs=pl.BlockSpec((group * copies, 3, rows, HD), lambda g: (g, 0, 0, 0)),
    )(queries, keys, values)


def body(queries, keys, values, gain_q, gain_k, w_latent, w_temporal, w_decode):
    devices = lax.axis_size("seq")
    copies = devices // HEADS
    rows = queries.shape[0]

    stacked = pack(queries, keys, values, copies)
    got = lax.all_to_all(stacked, "seq", split_axis=0, concat_axis=0, tiled=True)
    share = lax.axis_index("seq") % copies
    span_blocks = devices // copies
    out = attend(got, jnp.reshape(share, (1,)).astype(jnp.int32), span_blocks, gain_q, gain_k)
    if copies > 1:
        placed = jnp.zeros((copies, span_blocks, rows, HD), jnp.bfloat16)
        placed = lax.dynamic_update_index_in_dim(placed, out, share, 0)
        out = placed.reshape(devices, rows, HD)
    back = lax.all_to_all(out, "seq", split_axis=0, concat_axis=0, tiled=True)
    if copies > 1:
        back = jnp.sum(back.reshape(HEADS, copies, rows, HD).astype(jnp.float32), axis=1)
        back = back.astype(jnp.bfloat16)
    attention = jnp.transpose(back.reshape(HEADS, rows, HD), (1, 0, 2)).reshape(rows, HEADS * HD)
    latent = jnp.dot(attention, w_latent, preferred_element_type=jnp.float32).astype(jnp.bfloat16)
    earlier_one = passed_along(latent, "seq", 1)
    earlier_two = passed_along(latent, "seq", 2)
    state = jnp.dot(latent, w_temporal[0], preferred_element_type=jnp.float32)
    state = state + jnp.dot(earlier_one, w_temporal[1], preferred_element_type=jnp.float32)
    state = state + jnp.dot(earlier_two, w_temporal[2], preferred_element_type=jnp.float32)
    decoded = jnp.dot(
        jax.nn.silu(state).astype(jnp.bfloat16), w_decode, preferred_element_type=jnp.float32
    )
    return (attention, decoded.astype(jnp.bfloat16))


def solution(mesh):
    in_specs = (
        P(("groups", "seq"), None),
        P(("groups", "seq"), None),
        P(("groups", "seq"), None),
        P(),
        P(),
        P(),
        P(),
        P(),
    )
    out_specs = (P(("groups", "seq"), None), P(("groups", "seq"), None))
    return jax.shard_map(body, mesh=mesh, in_specs=in_specs, out_specs=out_specs, check_vma=False)
```

```python
import math

import jax
import jax.numpy as jnp
from jax import lax
from jax.experimental import pallas as pl
from jax.experimental.pallas import tpu as pltpu
from jax.sharding import PartitionSpec as P

HEADS = 16
HD = 128
EPS = 1e-06


def passed_along(shard, axis, by):
    peers = lax.axis_size(axis)
    pairs = [(i, i + by) for i in range(peers) if 0 <= i + by < peers]
    return lax.ppermute(shard, axis, pairs)


def _norm(x, gain):
    x = x.astype(jnp.float32)
    x = x * lax.rsqrt(jnp.mean(x * x, axis=-1, keepdims=True) + EPS) * gain
    return x.astype(jnp.bfloat16)


def _attn_kernel(share_ref, q_ref, k_ref, v_ref, gq_ref, gk_ref, o_ref, kn_ref):
    @pl.when(pl.program_id(0) == 0)
    def _():
        k = k_ref[...]
        k = k.reshape(k.shape[0] * k.shape[1], HD)
        kn_ref[...] = _norm(k, gk_ref[...])

    q = q_ref[...]
    q = q.reshape(q.shape[0] * q.shape[1], HD)
    qn = _norm(q, gq_ref[...])
    kn = kn_ref[...]
    v = v_ref[...]
    v = v.reshape(v.shape[0] * v.shape[1], HD)
    s = lax.dot_general(qn, kn, (((1,), (1,)), ((), ())), preferred_element_type=jnp.float32)
    c = math.log2(math.e) / math.sqrt(HD)
    m = jnp.max(s, axis=-1, keepdims=True)
    e = jnp.exp2(s * c - m * c)
    total = jnp.sum(e, axis=-1, keepdims=True)
    out = jnp.dot(e.astype(jnp.bfloat16), v, preferred_element_type=jnp.float32)
    out = (out / total).astype(jnp.bfloat16)
    o_ref[...] = out.reshape(o_ref.shape)


def attend(got, share, span_blocks, gain_q, gain_k, qb_rows=256):
    src, _, rows, _ = got.shape
    qb = max(1, qb_rows // rows)
    qb = min(qb, span_blocks)
    steps = span_blocks // qb
    tokens = src * rows
    return pl.pallas_call(
        _attn_kernel,
        out_shape=jax.ShapeDtypeStruct((span_blocks, rows, HD), jnp.bfloat16),
        grid_spec=pltpu.PrefetchScalarGridSpec(
            num_scalar_prefetch=1,
            grid=(steps,),
            in_specs=[
                pl.BlockSpec((qb, None, rows, HD), lambda i, sh: (sh[0] * steps + i, 0, 0, 0)),
                pl.BlockSpec((src, None, rows, HD), lambda i, sh: (0, 1, 0, 0)),
                pl.BlockSpec((src, None, rows, HD), lambda i, sh: (0, 2, 0, 0)),
                pl.BlockSpec((1, HD), lambda i, sh: (0, 0)),
                pl.BlockSpec((1, HD), lambda i, sh: (0, 0)),
            ],
            out_specs=pl.BlockSpec((qb, rows, HD), lambda i, sh: (i, 0, 0)),
            scratch_shapes=[pltpu.VMEM((tokens, HD), jnp.bfloat16)],
        ),
        compiler_params=pltpu.CompilerParams(
            dimension_semantics=("arbitrary",), vmem_limit_bytes=48 * 1024 * 1024
        ),
    )(share, got, got, got, gain_q.reshape(1, HD), gain_k.reshape(1, HD))


def _pack_kernel(q_ref, k_ref, v_ref, o_ref):
    group = q_ref.shape[1] // HD
    copies = o_ref.shape[0] // group
    for i in range(group):
        for c in range(copies):
            for j, ref in enumerate((q_ref, k_ref, v_ref)):
                o_ref[i * copies + c, j] = ref[:, i * HD:(i + 1) * HD]


def pack(queries, keys, values, copies):
    rows = queries.shape[0]
    group = 8
    spec = pl.BlockSpec((rows, group * HD), lambda g: (0, g))
    return pl.pallas_call(
        _pack_kernel,
        out_shape=jax.ShapeDtypeStruct((HEADS * copies, 3, rows, HD), jnp.bfloat16),
        grid=(HEADS // group,),
        in_specs=[spec, spec, spec],
        out_specs=pl.BlockSpec((group * copies, 3, rows, HD), lambda g: (g, 0, 0, 0)),
    )(queries, keys, values)


def _latent_kernel(b_ref, w_ref, z_ref):
    acc = jnp.zeros(z_ref.shape, jnp.float32)
    for h in range(b_ref.shape[0]):
        acc = acc + jnp.dot(b_ref[h], w_ref[h * HD:(h + 1) * HD, :], preferred_element_type=jnp.float32)
    z_ref[...] = acc.astype(z_ref.dtype)


def latent_of(back, w_latent):
    heads, rows, _ = back.shape
    return pl.pallas_call(
        _latent_kernel,
        out_shape=jax.ShapeDtypeStruct((rows, w_latent.shape[1]), jnp.bfloat16),
    )(back, w_latent)


def _decode_kernel(z_ref, e1_ref, e2_ref, wt_ref, wd_ref, o_ref):
    state = jnp.dot(z_ref[...], wt_ref[0], preferred_element_type=jnp.float32)
    state = state + jnp.dot(e1_ref[...], wt_ref[1], preferred_element_type=jnp.float32)
    state = state + jnp.dot(e2_ref[...], wt_ref[2], preferred_element_type=jnp.float32)
    act = jax.nn.silu(state).astype(jnp.bfloat16)
    o_ref[...] = jnp.dot(act, wd_ref[...], preferred_element_type=jnp.float32).astype(o_ref.dtype)


def decode(latent, earlier_one, earlier_two, w_temporal, w_decode):
    return pl.pallas_call(
        _decode_kernel,
        out_shape=jax.ShapeDtypeStruct((latent.shape[0], w_decode.shape[1]), jnp.bfloat16),
    )(latent, earlier_one, earlier_two, w_temporal, w_decode)


def body(queries, keys, values, gain_q, gain_k, w_latent, w_temporal, w_decode):
    devices = lax.axis_size("seq")
    copies = devices // HEADS
    rows = queries.shape[0]

    stacked = pack(queries, keys, values, copies)
    got = lax.all_to_all(stacked, "seq", split_axis=0, concat_axis=0, tiled=True)
    share = lax.axis_index("seq") % copies
    span_blocks = devices // copies
    out = attend(got, jnp.reshape(share, (1,)).astype(jnp.int32), span_blocks, gain_q, gain_k)
    if copies > 1:
        placed = jnp.zeros((copies, span_blocks, rows, HD), jnp.bfloat16)
        placed = lax.dynamic_update_index_in_dim(placed, out, share, 0)
        out = placed.reshape(devices, rows, HD)
    back = lax.all_to_all(out, "seq", split_axis=0, concat_axis=0, tiled=True)
    if copies > 1:
        back = jnp.sum(back.reshape(HEADS, copies, rows, HD).astype(jnp.float32), axis=1)
        back = back.astype(jnp.bfloat16)
    back = back.reshape(HEADS, rows, HD)
    latent = latent_of(back, w_latent)
    earlier_one = passed_along(latent, "seq", 1)
    earlier_two = passed_along(latent, "seq", 2)
    attention = jnp.transpose(back, (1, 0, 2)).reshape(rows, HEADS * HD)
    decoded = decode(latent, earlier_one, earlier_two, w_temporal, w_decode)
    return (attention, decoded)


def solution(mesh):
    in_specs = (
        P(("groups", "seq"), None),
        P(("groups", "seq"), None),
        P(("groups", "seq"), None),
        P(),
        P(),
        P(),
        P(),
        P(),
    )
    out_specs = (P(("groups", "seq"), None), P(("groups", "seq"), None))
    return jax.shard_map(body, mesh=mesh, in_specs=in_specs, out_specs=out_specs, check_vma=False)
```

```python
import math

import jax
import jax.numpy as jnp
from jax import lax
from jax.experimental import pallas as pl
from jax.experimental.pallas import tpu as pltpu
from jax.sharding import PartitionSpec as P

HEADS = 16
HD = 128
EPS = 1e-06


def passed_along(shard, axis, by):
    peers = lax.axis_size(axis)
    pairs = [(i, i + by) for i in range(peers) if 0 <= i + by < peers]
    return lax.ppermute(shard, axis, pairs)


def _norm(x, gain):
    x = x.astype(jnp.float32)
    x = x * lax.rsqrt(jnp.mean(x * x, axis=-1, keepdims=True) + EPS) * gain
    return x.astype(jnp.bfloat16)


def _attn_kernel(share_ref, q_ref, k_ref, v_ref, gq_ref, gk_ref, o_ref, kn_ref, vt_ref):
    @pl.when(pl.program_id(0) == 0)
    def _():
        k = k_ref[...]
        k = k.reshape(k.shape[0] * k.shape[1], HD)
        kn_ref[...] = _norm(k, gk_ref[...])
        v = v_ref[...]
        vt_ref[...] = v.reshape(v.shape[0] * v.shape[1], HD).T

    q = q_ref[...]
    q = q.reshape(q.shape[0] * q.shape[1], HD)
    qt = _norm(q, gq_ref[...]).T
    st = jnp.dot(kn_ref[...], qt, preferred_element_type=jnp.float32)
    c = math.log2(math.e) / math.sqrt(HD)
    m = jnp.max(st, axis=0, keepdims=True)
    e = jnp.exp2(st * c - m * c)
    total = jnp.sum(e, axis=0, keepdims=True)
    out_t = jnp.dot(vt_ref[...], e.astype(jnp.bfloat16), preferred_element_type=jnp.float32)
    out = (out_t / total).T.astype(jnp.bfloat16)
    o_ref[...] = out.reshape(o_ref.shape)


def attend(got, share, span_blocks, gain_q, gain_k):
    src, _, rows, _ = got.shape
    tokens = src * rows
    qb = max(1, min(span_blocks, (4 << 20) // (tokens * rows)))
    steps = span_blocks // qb
    tokens = src * rows
    return pl.pallas_call(
        _attn_kernel,
        out_shape=jax.ShapeDtypeStruct((span_blocks, rows, HD), jnp.bfloat16),
        grid_spec=pltpu.PrefetchScalarGridSpec(
            num_scalar_prefetch=1,
            grid=(steps,),
            in_specs=[
                pl.BlockSpec((qb, None, rows, HD), lambda i, sh: (sh[0] * steps + i, 0, 0, 0)),
                pl.BlockSpec((src, None, rows, HD), lambda i, sh: (0, 1, 0, 0)),
                pl.BlockSpec((src, None, rows, HD), lambda i, sh: (0, 2, 0, 0)),
                pl.BlockSpec((1, HD), lambda i, sh: (0, 0)),
                pl.BlockSpec((1, HD), lambda i, sh: (0, 0)),
            ],
            out_specs=pl.BlockSpec((qb, rows, HD), lambda i, sh: (i, 0, 0)),
            scratch_shapes=[pltpu.VMEM((tokens, HD), jnp.bfloat16), pltpu.VMEM((HD, tokens), jnp.bfloat16)],
        ),
        compiler_params=pltpu.CompilerParams(
            dimension_semantics=("arbitrary",), vmem_limit_bytes=48 * 1024 * 1024
        ),
    )(share, got, got, got, gain_q.reshape(1, HD), gain_k.reshape(1, HD))


def _pack_kernel(q_ref, k_ref, v_ref, o_ref):
    group = q_ref.shape[1] // HD
    copies = o_ref.shape[0] // group
    for i in range(group):
        for c in range(copies):
            for j, ref in enumerate((q_ref, k_ref, v_ref)):
                o_ref[i * copies + c, j] = ref[:, i * HD:(i + 1) * HD]


def pack(queries, keys, values, copies):
    rows = queries.shape[0]
    group = 8
    spec = pl.BlockSpec((rows, group * HD), lambda g: (0, g))
    return pl.pallas_call(
        _pack_kernel,
        out_shape=jax.ShapeDtypeStruct((HEADS * copies, 3, rows, HD), jnp.bfloat16),
        grid=(HEADS // group,),
        in_specs=[spec, spec, spec],
        out_specs=pl.BlockSpec((group * copies, 3, rows, HD), lambda g: (g, 0, 0, 0)),
    )(queries, keys, values)


def body(queries, keys, values, gain_q, gain_k, w_latent, w_temporal, w_decode):
    devices = lax.axis_size("seq")
    copies = devices // HEADS
    rows = queries.shape[0]

    stacked = pack(queries, keys, values, copies)
    got = lax.all_to_all(stacked, "seq", split_axis=0, concat_axis=0, tiled=True)
    share = lax.axis_index("seq") % copies
    span_blocks = devices // copies
    out = attend(got, jnp.reshape(share, (1,)).astype(jnp.int32), span_blocks, gain_q, gain_k)
    if copies > 1:
        placed = jnp.zeros((copies, span_blocks, rows, HD), jnp.bfloat16)
        placed = lax.dynamic_update_index_in_dim(placed, out, share, 0)
        out = placed.reshape(devices, rows, HD)
    back = lax.all_to_all(out, "seq", split_axis=0, concat_axis=0, tiled=True)
    if copies > 1:
        back = jnp.sum(back.reshape(HEADS, copies, rows, HD).astype(jnp.float32), axis=1)
        back = back.astype(jnp.bfloat16)
    attention = jnp.transpose(back.reshape(HEADS, rows, HD), (1, 0, 2)).reshape(rows, HEADS * HD)
    latent = jnp.dot(attention, w_latent, preferred_element_type=jnp.float32).astype(jnp.bfloat16)
    earlier_one = passed_along(latent, "seq", 1)
    earlier_two = passed_along(latent, "seq", 2)
    state = jnp.dot(latent, w_temporal[0], preferred_element_type=jnp.float32)
    state = state + jnp.dot(earlier_one, w_temporal[1], preferred_element_type=jnp.float32)
    state = state + jnp.dot(earlier_two, w_temporal[2], preferred_element_type=jnp.float32)
    decoded = jnp.dot(
        jax.nn.silu(state).astype(jnp.bfloat16), w_decode, preferred_element_type=jnp.float32
    )
    return (attention, decoded.astype(jnp.bfloat16))


def solution(mesh):
    in_specs = (
        P(("groups", "seq"), None),
        P(("groups", "seq"), None),
        P(("groups", "seq"), None),
        P(),
        P(),
        P(),
        P(),
        P(),
    )
    out_specs = (P(("groups", "seq"), None), P(("groups", "seq"), None))
    return jax.shard_map(body, mesh=mesh, in_specs=in_specs, out_specs=out_specs, check_vma=False)
```

```python
import math

import jax
import jax.numpy as jnp
from jax import lax
from jax.experimental import pallas as pl
from jax.experimental.pallas import tpu as pltpu
from jax.sharding import PartitionSpec as P

HEADS = 16
HD = 128
EPS = 1e-06


def passed_along(shard, axis, by):
    peers = lax.axis_size(axis)
    pairs = [(i, i + by) for i in range(peers) if 0 <= i + by < peers]
    return lax.ppermute(shard, axis, pairs)


def _norm(x, gain):
    x = x.astype(jnp.float32)
    x = x * lax.rsqrt(jnp.mean(x * x, axis=-1, keepdims=True) + EPS) * gain
    return x.astype(jnp.bfloat16)


def _attn_kernel(share_ref, q_ref, k_ref, v_ref, gq_ref, gk_ref, o_ref, kn_ref, vt_ref):
    @pl.when(pl.program_id(0) == 0)
    def _():
        k = k_ref[...]
        k = k.reshape(k.shape[0] * k.shape[1], HD)
        kn_ref[...] = _norm(k, gk_ref[...])
        v = v_ref[...]
        vt_ref[...] = v.reshape(v.shape[0] * v.shape[1], HD).T

    q = q_ref[...]
    q = q.reshape(q.shape[0] * q.shape[1], HD)
    qt = _norm(q, gq_ref[...]).T
    st = jnp.dot(kn_ref[...], qt, preferred_element_type=jnp.float32)
    c = math.log2(math.e) / math.sqrt(HD)
    m = jnp.max(st, axis=0, keepdims=True)
    e = jnp.exp2(st * c - m * c)
    total = jnp.sum(e, axis=0, keepdims=True)
    out_t = jnp.dot(vt_ref[...], e.astype(jnp.bfloat16), preferred_element_type=jnp.float32)
    out = (out_t / total).T.astype(jnp.bfloat16)
    o_ref[...] = out.reshape(o_ref.shape)


def attend(got, share, span_blocks, gain_q, gain_k):
    src, _, rows, _ = got.shape
    tokens = src * rows
    qb = max(1, min(span_blocks, (4 << 20) // (tokens * rows)))
    steps = span_blocks // qb
    tokens = src * rows
    return pl.pallas_call(
        _attn_kernel,
        out_shape=jax.ShapeDtypeStruct((span_blocks, rows, HD), jnp.bfloat16),
        grid_spec=pltpu.PrefetchScalarGridSpec(
            num_scalar_prefetch=1,
            grid=(steps,),
            in_specs=[
                pl.BlockSpec((qb, None, rows, HD), lambda i, sh: (sh[0] * steps + i, 0, 0, 0)),
                pl.BlockSpec((src, None, rows, HD), lambda i, sh: (0, 1, 0, 0)),
                pl.BlockSpec((src, None, rows, HD), lambda i, sh: (0, 2, 0, 0)),
                pl.BlockSpec((1, HD), lambda i, sh: (0, 0)),
                pl.BlockSpec((1, HD), lambda i, sh: (0, 0)),
            ],
            out_specs=pl.BlockSpec((qb, rows, HD), lambda i, sh: (i, 0, 0)),
            scratch_shapes=[pltpu.VMEM((tokens, HD), jnp.bfloat16), pltpu.VMEM((HD, tokens), jnp.bfloat16)],
        ),
        compiler_params=pltpu.CompilerParams(
            dimension_semantics=("arbitrary",), vmem_limit_bytes=48 * 1024 * 1024
        ),
    )(share, got, got, got, gain_q.reshape(1, HD), gain_k.reshape(1, HD))


def _pack_kernel(q_ref, k_ref, v_ref, o_ref):
    group = q_ref.shape[1] // HD
    copies = o_ref.shape[0] // group
    for i in range(group):
        for c in range(copies):
            for j, ref in enumerate((q_ref, k_ref, v_ref)):
                o_ref[i * copies + c, j] = ref[:, i * HD:(i + 1) * HD]


def pack(queries, keys, values, copies):
    rows = queries.shape[0]
    group = 8
    spec = pl.BlockSpec((rows, group * HD), lambda g: (0, g))
    return pl.pallas_call(
        _pack_kernel,
        out_shape=jax.ShapeDtypeStruct((HEADS * copies, 3, rows, HD), jnp.bfloat16),
        grid=(HEADS // group,),
        in_specs=[spec, spec, spec],
        out_specs=pl.BlockSpec((group * copies, 3, rows, HD), lambda g: (g, 0, 0, 0)),
    )(queries, keys, values)


def body(queries, keys, values, gain_q, gain_k, w_latent, w_temporal, w_decode):
    devices = lax.axis_size("seq")
    copies = devices // HEADS
    rows = queries.shape[0]

    stacked = pack(queries, keys, values, copies)
    got = lax.all_to_all(stacked, "seq", split_axis=0, concat_axis=0, tiled=True)
    share = lax.axis_index("seq") % copies
    span_blocks = devices // copies
    out = attend(got, jnp.reshape(share, (1,)).astype(jnp.int32), span_blocks, gain_q, gain_k)
    if copies > 1:
        placed = jnp.zeros((copies, span_blocks, rows, HD), jnp.bfloat16)
        placed = lax.dynamic_update_index_in_dim(placed, out, share, 0)
        out = placed.reshape(devices, rows, HD)
    back = lax.all_to_all(out, "seq", split_axis=0, concat_axis=0, tiled=True)
    if copies > 1:
        back = jnp.sum(back.reshape(HEADS, copies, rows, HD).astype(jnp.float32), axis=1)
        back = back.astype(jnp.bfloat16)
    back = back.reshape(HEADS, rows, HD)
    latent = jnp.einsum(
        "hrd,hdc->rc", back, w_latent.reshape(HEADS, HD, -1), preferred_element_type=jnp.float32
    ).astype(jnp.bfloat16)
    attention = jnp.transpose(back, (1, 0, 2)).reshape(rows, HEADS * HD)
    earlier_one = passed_along(latent, "seq", 1)
    earlier_two = passed_along(latent, "seq", 2)
    state = jnp.dot(latent, w_temporal[0], preferred_element_type=jnp.float32)
    state = state + jnp.dot(earlier_one, w_temporal[1], preferred_element_type=jnp.float32)
    state = state + jnp.dot(earlier_two, w_temporal[2], preferred_element_type=jnp.float32)
    act = lax.optimization_barrier(jax.nn.silu(state).astype(jnp.bfloat16))
    decoded = jnp.dot(act, w_decode, preferred_element_type=jnp.float32)
    return (attention, decoded.astype(jnp.bfloat16))


def solution(mesh):
    in_specs = (
        P(("groups", "seq"), None),
        P(("groups", "seq"), None),
        P(("groups", "seq"), None),
        P(),
        P(),
        P(),
        P(),
        P(),
    )
    out_specs = (P(("groups", "seq"), None), P(("groups", "seq"), None))
    return jax.shard_map(body, mesh=mesh, in_specs=in_specs, out_specs=out_specs, check_vma=False)
```

```python
import math

import jax
import jax.numpy as jnp
from jax import lax
from jax.experimental import pallas as pl
from jax.experimental.pallas import tpu as pltpu
from jax.sharding import PartitionSpec as P

HEADS = 16
HD = 128
EPS = 1e-06


def passed_along(shard, axis, by):
    peers = lax.axis_size(axis)
    pairs = [(i, i + by) for i in range(peers) if 0 <= i + by < peers]
    return lax.ppermute(shard, axis, pairs)


def _norm(x, gain):
    x = x.astype(jnp.float32)
    x = x * lax.rsqrt(jnp.mean(x * x, axis=-1, keepdims=True) + EPS) * gain
    return x.astype(jnp.bfloat16)


def _attn_kernel(share_ref, q_ref, k_ref, v_ref, gq_ref, gk_ref, o_ref, kn_ref, vt_ref):
    @pl.when(pl.program_id(0) == 0)
    def _():
        k = k_ref[...]
        k = k.reshape(k.shape[0] * k.shape[1], HD)
        kn_ref[...] = _norm(k, gk_ref[...])
        v = v_ref[...]
        vt_ref[...] = v.reshape(v.shape[0] * v.shape[1], HD).T

    q = q_ref[...]
    q = q.reshape(q.shape[0] * q.shape[1], HD)
    qt = _norm(q, gq_ref[...]).T
    st = jnp.dot(kn_ref[...], qt, preferred_element_type=jnp.float32)
    c = math.log2(math.e) / math.sqrt(HD)
    m = jnp.max(st, axis=0, keepdims=True)
    e = jnp.exp2(st * c - m * c)
    total = jnp.sum(e, axis=0, keepdims=True)
    out_t = jnp.dot(vt_ref[...], e.astype(jnp.bfloat16), preferred_element_type=jnp.float32)
    out = (out_t / total).T.astype(jnp.bfloat16)
    o_ref[...] = out.reshape(o_ref.shape)


def attend(got, share, span_blocks, gain_q, gain_k):
    src, _, rows, _ = got.shape
    tokens = src * rows
    qb = max(1, min(span_blocks, (4 << 20) // (tokens * rows)))
    steps = span_blocks // qb
    tokens = src * rows
    return pl.pallas_call(
        _attn_kernel,
        out_shape=jax.ShapeDtypeStruct((span_blocks, rows, HD), jnp.bfloat16),
        grid_spec=pltpu.PrefetchScalarGridSpec(
            num_scalar_prefetch=1,
            grid=(steps,),
            in_specs=[
                pl.BlockSpec((qb, None, rows, HD), lambda i, sh: (sh[0] * steps + i, 0, 0, 0)),
                pl.BlockSpec((src, None, rows, HD), lambda i, sh: (0, 1, 0, 0)),
                pl.BlockSpec((src, None, rows, HD), lambda i, sh: (0, 2, 0, 0)),
                pl.BlockSpec((1, HD), lambda i, sh: (0, 0)),
                pl.BlockSpec((1, HD), lambda i, sh: (0, 0)),
            ],
            out_specs=pl.BlockSpec((qb, rows, HD), lambda i, sh: (i, 0, 0)),
            scratch_shapes=[pltpu.VMEM((tokens, HD), jnp.bfloat16), pltpu.VMEM((HD, tokens), jnp.bfloat16)],
        ),
        compiler_params=pltpu.CompilerParams(
            dimension_semantics=("arbitrary",), vmem_limit_bytes=48 * 1024 * 1024
        ),
    )(share, got, got, got, gain_q.reshape(1, HD), gain_k.reshape(1, HD))


def _pack_kernel(q_ref, k_ref, v_ref, o_ref):
    group = q_ref.shape[1] // HD
    copies = o_ref.shape[0] // group
    for i in range(group):
        for c in range(copies):
            for j, ref in enumerate((q_ref, k_ref, v_ref)):
                o_ref[i * copies + c, j] = ref[:, i * HD:(i + 1) * HD]


def pack(queries, keys, values, copies):
    rows = queries.shape[0]
    group = 8
    spec = pl.BlockSpec((rows, group * HD), lambda g: (0, g))
    return pl.pallas_call(
        _pack_kernel,
        out_shape=jax.ShapeDtypeStruct((HEADS * copies, 3, rows, HD), jnp.bfloat16),
        grid=(HEADS // group,),
        in_specs=[spec, spec, spec],
        out_specs=pl.BlockSpec((group * copies, 3, rows, HD), lambda g: (g, 0, 0, 0)),
    )(queries, keys, values)


def _decode_kernel(z_ref, e1_ref, e2_ref, wt_ref, wd_ref, o_ref):
    state = jnp.dot(z_ref[...], wt_ref[0], preferred_element_type=jnp.float32)
    state = state + jnp.dot(e1_ref[...], wt_ref[1], preferred_element_type=jnp.float32)
    state = state + jnp.dot(e2_ref[...], wt_ref[2], preferred_element_type=jnp.float32)
    act = jax.nn.silu(state).astype(jnp.bfloat16)
    o_ref[...] = jnp.dot(act, wd_ref[...], preferred_element_type=jnp.float32).astype(o_ref.dtype)


def decode(latent, earlier_one, earlier_two, w_temporal, w_decode):
    vmem = pl.BlockSpec(memory_space=pltpu.VMEM)
    return pl.pallas_call(
        _decode_kernel,
        out_shape=jax.ShapeDtypeStruct((latent.shape[0], w_decode.shape[1]), jnp.bfloat16),
        in_specs=[vmem] * 5,
        out_specs=vmem,
    )(latent, earlier_one, earlier_two, w_temporal, w_decode)


def body(queries, keys, values, gain_q, gain_k, w_latent, w_temporal, w_decode):
    devices = lax.axis_size("seq")
    copies = devices // HEADS
    rows = queries.shape[0]

    stacked = pack(queries, keys, values, copies)
    got = lax.all_to_all(stacked, "seq", split_axis=0, concat_axis=0, tiled=True)
    share = lax.axis_index("seq") % copies
    span_blocks = devices // copies
    out = attend(got, jnp.reshape(share, (1,)).astype(jnp.int32), span_blocks, gain_q, gain_k)
    if copies > 1:
        placed = jnp.zeros((copies, span_blocks, rows, HD), jnp.bfloat16)
        placed = lax.dynamic_update_index_in_dim(placed, out, share, 0)
        out = placed.reshape(devices, rows, HD)
    back = lax.all_to_all(out, "seq", split_axis=0, concat_axis=0, tiled=True)
    if copies > 1:
        back = jnp.sum(back.reshape(HEADS, copies, rows, HD).astype(jnp.float32), axis=1)
        back = back.astype(jnp.bfloat16)
    back = back.reshape(HEADS, rows, HD)
    latent = jnp.einsum(
        "hrd,hdc->rc", back, w_latent.reshape(HEADS, HD, -1), preferred_element_type=jnp.float32
    ).astype(jnp.bfloat16)
    attention = jnp.transpose(back, (1, 0, 2)).reshape(rows, HEADS * HD)
    earlier_one = passed_along(latent, "seq", 1)
    earlier_two = passed_along(latent, "seq", 2)
    decoded = decode(latent, earlier_one, earlier_two, w_temporal, w_decode)
    return (attention, decoded)


def solution(mesh):
    in_specs = (
        P(("groups", "seq"), None),
        P(("groups", "seq"), None),
        P(("groups", "seq"), None),
        P(),
        P(),
        P(),
        P(),
        P(),
    )
    out_specs = (P(("groups", "seq"), None), P(("groups", "seq"), None))
    return jax.shard_map(body, mesh=mesh, in_specs=in_specs, out_specs=out_specs, check_vma=False)
```

```python
import math

import jax
import jax.numpy as jnp
from jax import lax
from jax.experimental import pallas as pl
from jax.experimental.pallas import tpu as pltpu
from jax.sharding import PartitionSpec as P

HEADS = 16
HD = 128
EPS = 1e-06


def passed_along(shard, axis, by):
    peers = lax.axis_size(axis)
    pairs = [(i, i + by) for i in range(peers) if 0 <= i + by < peers]
    return lax.ppermute(shard, axis, pairs)


def _norm(x, gain):
    x = x.astype(jnp.float32)
    x = x * lax.rsqrt(jnp.mean(x * x, axis=-1, keepdims=True) + EPS) * gain
    return x.astype(jnp.bfloat16)


def _attn_kernel(share_ref, q_ref, k_ref, v_ref, gq_ref, gk_ref, o_ref, kn_ref, vt_ref):
    @pl.when(pl.program_id(0) == 0)
    def _():
        k = k_ref[...]
        k = k.reshape(k.shape[0] * k.shape[1], HD)
        kn_ref[...] = _norm(k, gk_ref[...])
        v = v_ref[...]
        vt_ref[...] = v.reshape(v.shape[0] * v.shape[1], HD).T

    q = q_ref[...]
    q = q.reshape(q.shape[0] * q.shape[1], HD)
    qt = _norm(q, gq_ref[...]).T
    st = jnp.dot(kn_ref[...], qt, preferred_element_type=jnp.float32)
    c = math.log2(math.e) / math.sqrt(HD)
    m = jnp.max(st, axis=0, keepdims=True)
    e = jnp.exp2(st * c - m * c)
    total = jnp.sum(e, axis=0, keepdims=True)
    out_t = jnp.dot(vt_ref[...], e.astype(jnp.bfloat16), preferred_element_type=jnp.float32)
    out = (out_t / total).T.astype(jnp.bfloat16)
    o_ref[...] = out.reshape(o_ref.shape)


def attend(got, share, span_blocks, gain_q, gain_k):
    src, _, rows, _ = got.shape
    tokens = src * rows
    qb = max(1, min(span_blocks, (4 << 20) // (tokens * rows)))
    steps = span_blocks // qb
    tokens = src * rows
    return pl.pallas_call(
        _attn_kernel,
        out_shape=jax.ShapeDtypeStruct((span_blocks, rows, HD), jnp.bfloat16),
        grid_spec=pltpu.PrefetchScalarGridSpec(
            num_scalar_prefetch=1,
            grid=(steps,),
            in_specs=[
                pl.BlockSpec((qb, None, rows, HD), lambda i, sh: (sh[0] * steps + i, 0, 0, 0)),
                pl.BlockSpec((src, None, rows, HD), lambda i, sh: (0, 1, 0, 0)),
                pl.BlockSpec((src, None, rows, HD), lambda i, sh: (0, 2, 0, 0)),
                pl.BlockSpec((1, HD), lambda i, sh: (0, 0)),
                pl.BlockSpec((1, HD), lambda i, sh: (0, 0)),
            ],
            out_specs=pl.BlockSpec((qb, rows, HD), lambda i, sh: (i, 0, 0)),
            scratch_shapes=[pltpu.VMEM((tokens, HD), jnp.bfloat16), pltpu.VMEM((HD, tokens), jnp.bfloat16)],
        ),
        compiler_params=pltpu.CompilerParams(
            dimension_semantics=("arbitrary",), vmem_limit_bytes=48 * 1024 * 1024
        ),
    )(share, got, got, got, gain_q.reshape(1, HD), gain_k.reshape(1, HD))


def _pack_kernel(q_ref, k_ref, v_ref, o_ref):
    group = q_ref.shape[1] // HD
    copies = o_ref.shape[0] // group
    for i in range(group):
        for c in range(copies):
            for j, ref in enumerate((q_ref, k_ref, v_ref)):
                o_ref[i * copies + c, j] = ref[:, i * HD:(i + 1) * HD]


def pack(queries, keys, values, copies):
    rows = queries.shape[0]
    group = 8
    spec = pl.BlockSpec((rows, group * HD), lambda g: (0, g))
    return pl.pallas_call(
        _pack_kernel,
        out_shape=jax.ShapeDtypeStruct((HEADS * copies, 3, rows, HD), jnp.bfloat16),
        grid=(HEADS // group,),
        in_specs=[spec, spec, spec],
        out_specs=pl.BlockSpec((group * copies, 3, rows, HD), lambda g: (g, 0, 0, 0)),
    )(queries, keys, values)


def body(queries, keys, values, gain_q, gain_k, w_latent, w_temporal, w_decode):
    devices = lax.axis_size("seq")
    copies = devices // HEADS
    rows = queries.shape[0]

    stacked = pack(queries, keys, values, copies)
    got = lax.all_to_all(stacked, "seq", split_axis=0, concat_axis=0, tiled=True)
    share = lax.axis_index("seq") % copies
    span_blocks = devices // copies
    out = attend(got, jnp.reshape(share, (1,)).astype(jnp.int32), span_blocks, gain_q, gain_k)
    if copies > 1:
        placed = jnp.zeros((copies, span_blocks, rows, HD), jnp.bfloat16)
        placed = lax.dynamic_update_index_in_dim(placed, out, share, 0)
        out = placed.reshape(devices, rows, HD)
    back = lax.all_to_all(out, "seq", split_axis=0, concat_axis=0, tiled=True)
    if copies > 1:
        back = jnp.sum(back.reshape(HEADS, copies, rows, HD).astype(jnp.float32), axis=1)
        back = back.astype(jnp.bfloat16)
    back = back.reshape(HEADS, rows, HD)
    latent = jnp.einsum(
        "hrd,hdc->rc", back, w_latent.reshape(HEADS, HD, -1), preferred_element_type=jnp.float32
    ).astype(jnp.bfloat16)
    attention = jnp.transpose(back, (1, 0, 2)).reshape(rows, HEADS * HD)
    earlier_one = passed_along(latent, "seq", 1)
    earlier_two = passed_along(latent, "seq", 2)
    taps = jnp.concatenate([latent, earlier_one, earlier_two], axis=1)
    state = jnp.dot(taps, w_temporal.reshape(-1, w_temporal.shape[2]), preferred_element_type=jnp.float32)
    act = lax.optimization_barrier(jax.nn.silu(state).astype(jnp.bfloat16))
    decoded = jnp.dot(act, w_decode, preferred_element_type=jnp.float32).astype(jnp.bfloat16)
    return (attention, decoded)


def solution(mesh):
    in_specs = (
        P(("groups", "seq"), None),
        P(("groups", "seq"), None),
        P(("groups", "seq"), None),
        P(),
        P(),
        P(),
        P(),
        P(),
    )
    out_specs = (P(("groups", "seq"), None), P(("groups", "seq"), None))
    return jax.shard_map(body, mesh=mesh, in_specs=in_specs, out_specs=out_specs, check_vma=False)
```

```python
import math

import jax
import jax.numpy as jnp
from jax import lax
from jax.experimental import pallas as pl
from jax.experimental.pallas import tpu as pltpu
from jax.sharding import PartitionSpec as P

HEADS = 16
HD = 128
EPS = 1e-06


def passed_along(shard, axis, by):
    peers = lax.axis_size(axis)
    pairs = [(i, i + by) for i in range(peers) if 0 <= i + by < peers]
    return lax.ppermute(shard, axis, pairs)


def _norm(x, gain):
    x = x.astype(jnp.float32)
    x = x * lax.rsqrt(jnp.mean(x * x, axis=-1, keepdims=True) + EPS) * gain
    return x.astype(jnp.bfloat16)


def _attn_kernel(share_ref, q_ref, k_ref, v_ref, gq_ref, gk_ref, o_ref, kn_ref, vt_ref):
    @pl.when(pl.program_id(0) == 0)
    def _():
        k = k_ref[...]
        k = k.reshape(k.shape[0] * k.shape[1], HD)
        kn_ref[...] = _norm(k, gk_ref[...])
        v = v_ref[...]
        vt_ref[...] = v.reshape(v.shape[0] * v.shape[1], HD).T

    q = q_ref[...]
    q = q.reshape(q.shape[0] * q.shape[1], HD)
    qt = _norm(q, gq_ref[...]).T
    st = jnp.dot(kn_ref[...], qt, preferred_element_type=jnp.float32)
    c = math.log2(math.e) / math.sqrt(HD)
    m = jnp.max(st, axis=0, keepdims=True)
    e = jnp.exp2(st * c - m * c)
    total = jnp.sum(e, axis=0, keepdims=True)
    out_t = jnp.dot(vt_ref[...], e.astype(jnp.bfloat16), preferred_element_type=jnp.float32)
    out = (out_t / total).T.astype(jnp.bfloat16)
    o_ref[...] = out.reshape(o_ref.shape)


def attend(got, share, span_blocks, gain_q, gain_k):
    src, _, rows, _ = got.shape
    tokens = src * rows
    qb = max(1, min(span_blocks, (4 << 20) // (tokens * rows)))
    steps = span_blocks // qb
    tokens = src * rows
    return pl.pallas_call(
        _attn_kernel,
        out_shape=jax.ShapeDtypeStruct((span_blocks, rows, HD), jnp.bfloat16),
        grid_spec=pltpu.PrefetchScalarGridSpec(
            num_scalar_prefetch=1,
            grid=(steps,),
            in_specs=[
                pl.BlockSpec((qb, None, rows, HD), lambda i, sh: (sh[0] * steps + i, 0, 0, 0)),
                pl.BlockSpec((src, None, rows, HD), lambda i, sh: (0, 1, 0, 0)),
                pl.BlockSpec((src, None, rows, HD), lambda i, sh: (0, 2, 0, 0)),
                pl.BlockSpec((1, HD), lambda i, sh: (0, 0)),
                pl.BlockSpec((1, HD), lambda i, sh: (0, 0)),
            ],
            out_specs=pl.BlockSpec((qb, rows, HD), lambda i, sh: (i, 0, 0)),
            scratch_shapes=[pltpu.VMEM((tokens, HD), jnp.bfloat16), pltpu.VMEM((HD, tokens), jnp.bfloat16)],
        ),
        compiler_params=pltpu.CompilerParams(
            dimension_semantics=("arbitrary",), vmem_limit_bytes=48 * 1024 * 1024
        ),
    )(share, got, got, got, gain_q.reshape(1, HD), gain_k.reshape(1, HD))


def _pack_kernel(q_ref, k_ref, v_ref, o_ref):
    group = q_ref.shape[1] // HD
    copies = o_ref.shape[0] // group
    for i in range(group):
        for c in range(copies):
            for j, ref in enumerate((q_ref, k_ref, v_ref)):
                o_ref[i * copies + c, j] = ref[:, i * HD:(i + 1) * HD]


def pack(queries, keys, values, copies):
    rows = queries.shape[0]
    group = 8
    spec = pl.BlockSpec((rows, group * HD), lambda g: (0, g))
    return pl.pallas_call(
        _pack_kernel,
        out_shape=jax.ShapeDtypeStruct((HEADS * copies, 3, rows, HD), jnp.bfloat16),
        grid=(HEADS // group,),
        in_specs=[spec, spec, spec],
        out_specs=pl.BlockSpec((group * copies, 3, rows, HD), lambda g: (g, 0, 0, 0)),
    )(queries, keys, values)


def body(queries, keys, values, gain_q, gain_k, w_latent, w_temporal, w_decode):
    devices = lax.axis_size("seq")
    copies = devices // HEADS
    rows = queries.shape[0]

    stacked = pack(queries, keys, values, copies)
    got = lax.all_to_all(stacked, "seq", split_axis=0, concat_axis=0, tiled=True)
    share = lax.axis_index("seq") % copies
    span_blocks = devices // copies
    out = attend(got, jnp.reshape(share, (1,)).astype(jnp.int32), span_blocks, gain_q, gain_k)
    if copies > 1:
        placed = jnp.zeros((copies, span_blocks, rows, HD), jnp.bfloat16)
        placed = lax.dynamic_update_index_in_dim(placed, out, share, 0)
        out = placed.reshape(devices, rows, HD)
    back = lax.all_to_all(out, "seq", split_axis=0, concat_axis=0, tiled=True)
    if copies > 1:
        back = jnp.sum(back.reshape(HEADS, copies, rows, HD).astype(jnp.float32), axis=1)
        back = back.astype(jnp.bfloat16)
    back = back.reshape(HEADS, rows, HD)
    latent = jnp.einsum(
        "hrd,hdc->rc", back, w_latent.reshape(HEADS, HD, -1), preferred_element_type=jnp.float32
    ).astype(jnp.bfloat16)
    attention = jnp.transpose(back, (1, 0, 2)).reshape(rows, HEADS * HD)
    earlier_one = passed_along(latent, "seq", 1)
    earlier_two = passed_along(latent, "seq", 2)
    own = jnp.dot(latent, w_temporal[0], preferred_element_type=jnp.float32)
    own = lax.optimization_barrier(own)
    taps = jnp.concatenate([earlier_one, earlier_two], axis=1)
    state = own + jnp.dot(taps, w_temporal[1:].reshape(-1, w_temporal.shape[2]), preferred_element_type=jnp.float32)
    act = lax.optimization_barrier(jax.nn.silu(state).astype(jnp.bfloat16))
    decoded = jnp.dot(act, w_decode, preferred_element_type=jnp.float32).astype(jnp.bfloat16)
    return (attention, decoded)


def solution(mesh):
    in_specs = (
        P(("groups", "seq"), None),
        P(("groups", "seq"), None),
        P(("groups", "seq"), None),
        P(),
        P(),
        P(),
        P(),
        P(),
    )
    out_specs = (P(("groups", "seq"), None), P(("groups", "seq"), None))
    return jax.shard_map(body, mesh=mesh, in_specs=in_specs, out_specs=out_specs, check_vma=False)
```

```python
import math

import jax
import jax.numpy as jnp
from jax import lax
from jax.experimental import pallas as pl
from jax.experimental.pallas import tpu as pltpu
from jax.sharding import PartitionSpec as P

HEADS = 16
HD = 128
EPS = 1e-06


def passed_along(shard, axis, by):
    peers = lax.axis_size(axis)
    pairs = [(i, i + by) for i in range(peers) if 0 <= i + by < peers]
    return lax.ppermute(shard, axis, pairs)


def _norm(x, gain):
    x = x.astype(jnp.float32)
    x = x * lax.rsqrt(jnp.mean(x * x, axis=-1, keepdims=True) + EPS) * gain
    return x.astype(jnp.bfloat16)


def _attn_kernel(share_ref, q_ref, k_ref, v_ref, gq_ref, gk_ref, o_ref, kn_ref, vt_ref):
    @pl.when(pl.program_id(0) == 0)
    def _():
        k = k_ref[...]
        k = k.reshape(k.shape[0] * k.shape[1], HD)
        kn_ref[...] = _norm(k, gk_ref[...])
        v = v_ref[...]
        vt_ref[...] = v.reshape(v.shape[0] * v.shape[1], HD).T

    q = q_ref[...]
    q = q.reshape(q.shape[0] * q.shape[1], HD)
    qt = _norm(q, gq_ref[...]).T
    st = jnp.dot(kn_ref[...], qt, preferred_element_type=jnp.float32)
    c = math.log2(math.e) / math.sqrt(HD)
    m = jnp.max(st, axis=0, keepdims=True)
    e = jnp.exp2(st * c - m * c)
    total = jnp.sum(e, axis=0, keepdims=True)
    out_t = jnp.dot(vt_ref[...], e.astype(jnp.bfloat16), preferred_element_type=jnp.float32)
    out = (out_t / total).T.astype(jnp.bfloat16)
    o_ref[...] = out.reshape(o_ref.shape)


def attend(got, share, span_blocks, gain_q, gain_k):
    src, _, rows, _ = got.shape
    tokens = src * rows
    qb = max(1, min(span_blocks, (4 << 20) // (tokens * rows)))
    steps = span_blocks // qb
    tokens = src * rows
    return pl.pallas_call(
        _attn_kernel,
        out_shape=jax.ShapeDtypeStruct((span_blocks, rows, HD), jnp.bfloat16),
        grid_spec=pltpu.PrefetchScalarGridSpec(
            num_scalar_prefetch=1,
            grid=(steps,),
            in_specs=[
                pl.BlockSpec((qb, None, rows, HD), lambda i, sh: (sh[0] * steps + i, 0, 0, 0)),
                pl.BlockSpec((src, None, rows, HD), lambda i, sh: (0, 1, 0, 0)),
                pl.BlockSpec((src, None, rows, HD), lambda i, sh: (0, 2, 0, 0)),
                pl.BlockSpec((1, HD), lambda i, sh: (0, 0)),
                pl.BlockSpec((1, HD), lambda i, sh: (0, 0)),
            ],
            out_specs=pl.BlockSpec((qb, rows, HD), lambda i, sh: (i, 0, 0)),
            scratch_shapes=[pltpu.VMEM((tokens, HD), jnp.bfloat16), pltpu.VMEM((HD, tokens), jnp.bfloat16)],
        ),
        compiler_params=pltpu.CompilerParams(
            dimension_semantics=("arbitrary",), vmem_limit_bytes=48 * 1024 * 1024
        ),
    )(share, got, got, got, gain_q.reshape(1, HD), gain_k.reshape(1, HD))


def _pack_kernel(q_ref, k_ref, v_ref, o_ref):
    group = q_ref.shape[1] // HD
    copies = o_ref.shape[0] // group
    for i in range(group):
        for c in range(copies):
            for j, ref in enumerate((q_ref, k_ref, v_ref)):
                o_ref[i * copies + c, j] = ref[:, i * HD:(i + 1) * HD]


def pack(queries, keys, values, copies):
    rows = queries.shape[0]
    group = 8
    spec = pl.BlockSpec((rows, group * HD), lambda g: (0, g))
    return pl.pallas_call(
        _pack_kernel,
        out_shape=jax.ShapeDtypeStruct((HEADS * copies, 3, rows, HD), jnp.bfloat16),
        grid=(HEADS // group,),
        in_specs=[spec, spec, spec],
        out_specs=pl.BlockSpec((group * copies, 3, rows, HD), lambda g: (g, 0, 0, 0)),
    )(queries, keys, values)


def _unpack_kernel(b_ref, o_ref):
    for h in range(b_ref.shape[0]):
        o_ref[:, h * HD:(h + 1) * HD] = b_ref[h]


def unpack(back):
    heads, rows, _ = back.shape
    group = 8
    return pl.pallas_call(
        _unpack_kernel,
        out_shape=jax.ShapeDtypeStruct((rows, heads * HD), back.dtype),
        grid=(heads // group,),
        in_specs=[pl.BlockSpec((group, rows, HD), lambda g: (g, 0, 0))],
        out_specs=pl.BlockSpec((rows, group * HD), lambda g: (0, g)),
    )(back)


def body(queries, keys, values, gain_q, gain_k, w_latent, w_temporal, w_decode):
    devices = lax.axis_size("seq")
    copies = devices // HEADS
    rows = queries.shape[0]

    stacked = pack(queries, keys, values, copies)
    got = lax.all_to_all(stacked, "seq", split_axis=0, concat_axis=0, tiled=True)
    share = lax.axis_index("seq") % copies
    span_blocks = devices // copies
    out = attend(got, jnp.reshape(share, (1,)).astype(jnp.int32), span_blocks, gain_q, gain_k)
    if copies > 1:
        placed = jnp.zeros((copies, span_blocks, rows, HD), jnp.bfloat16)
        placed = lax.dynamic_update_index_in_dim(placed, out, share, 0)
        out = placed.reshape(devices, rows, HD)
    back = lax.all_to_all(out, "seq", split_axis=0, concat_axis=0, tiled=True)
    if copies > 1:
        back = jnp.sum(back.reshape(HEADS, copies, rows, HD).astype(jnp.float32), axis=1)
        back = back.astype(jnp.bfloat16)
    back = back.reshape(HEADS, rows, HD)
    latent = jnp.einsum(
        "hrd,hdc->rc", back, w_latent.reshape(HEADS, HD, -1), preferred_element_type=jnp.float32
    ).astype(jnp.bfloat16)
    attention = unpack(back)
    earlier_one = passed_along(latent, "seq", 1)
    earlier_two = passed_along(latent, "seq", 2)
    taps = jnp.concatenate([latent, earlier_one, earlier_two], axis=1)
    state = jnp.dot(taps, w_temporal.reshape(-1, w_temporal.shape[2]), preferred_element_type=jnp.float32)
    act = lax.optimization_barrier(jax.nn.silu(state).astype(jnp.bfloat16))
    decoded = jnp.dot(act, w_decode, preferred_element_type=jnp.float32).astype(jnp.bfloat16)
    return (attention, decoded)


def solution(mesh):
    in_specs = (
        P(("groups", "seq"), None),
        P(("groups", "seq"), None),
        P(("groups", "seq"), None),
        P(),
        P(),
        P(),
        P(),
        P(),
    )
    out_specs = (P(("groups", "seq"), None), P(("groups", "seq"), None))
    return jax.shard_map(body, mesh=mesh, in_specs=in_specs, out_specs=out_specs, check_vma=False)
```

```python
import math

import jax
import jax.numpy as jnp
from jax import lax
from jax.experimental import pallas as pl
from jax.experimental.pallas import tpu as pltpu
from jax.sharding import PartitionSpec as P

HEADS = 16
HD = 128
EPS = 1e-06


def passed_along(shard, axis, by):
    peers = lax.axis_size(axis)
    pairs = [(i, i + by) for i in range(peers) if 0 <= i + by < peers]
    return lax.ppermute(shard, axis, pairs)


def _norm(x, gain):
    x = x.astype(jnp.float32)
    x = x * lax.rsqrt(jnp.mean(x * x, axis=-1, keepdims=True) + EPS) * gain
    return x.astype(jnp.bfloat16)


def _attn_kernel(share_ref, q_ref, k_ref, v_ref, gq_ref, gk_ref, o_ref, kn_ref, vt_ref):
    @pl.when(pl.program_id(0) == 0)
    def _():
        k = k_ref[...]
        k = k.reshape(k.shape[0] * k.shape[1], HD)
        kn_ref[...] = _norm(k, gk_ref[...])
        v = v_ref[...]
        vt_ref[...] = v.reshape(v.shape[0] * v.shape[1], HD).T

    q = q_ref[...]
    q = q.reshape(q.shape[0] * q.shape[1], HD)
    qt = _norm(q, gq_ref[...]).T
    st = jnp.dot(kn_ref[...], qt, preferred_element_type=jnp.float32)
    c = math.log2(math.e) / math.sqrt(HD)
    m = jnp.max(st, axis=0, keepdims=True)
    e = jnp.exp2(st * c - m * c)
    total = jnp.sum(e, axis=0, keepdims=True)
    out_t = jnp.dot(vt_ref[...], e.astype(jnp.bfloat16), preferred_element_type=jnp.float32)
    out = (out_t / total).T.astype(jnp.bfloat16)
    o_ref[...] = out.reshape(o_ref.shape)


def attend(got, share, span_blocks, gain_q, gain_k):
    src, _, rows, _ = got.shape
    tokens = src * rows
    qb = max(1, min(span_blocks, (4 << 20) // (tokens * rows)))
    steps = span_blocks // qb
    tokens = src * rows
    return pl.pallas_call(
        _attn_kernel,
        out_shape=jax.ShapeDtypeStruct((span_blocks, rows, HD), jnp.bfloat16),
        grid_spec=pltpu.PrefetchScalarGridSpec(
            num_scalar_prefetch=1,
            grid=(steps,),
            in_specs=[
                pl.BlockSpec((qb, None, rows, HD), lambda i, sh: (sh[0] * steps + i, 0, 0, 0)),
                pl.BlockSpec((src, None, rows, HD), lambda i, sh: (0, 1, 0, 0)),
                pl.BlockSpec((src, None, rows, HD), lambda i, sh: (0, 2, 0, 0)),
                pl.BlockSpec((1, HD), lambda i, sh: (0, 0)),
                pl.BlockSpec((1, HD), lambda i, sh: (0, 0)),
            ],
            out_specs=pl.BlockSpec((qb, rows, HD), lambda i, sh: (i, 0, 0)),
            scratch_shapes=[pltpu.VMEM((tokens, HD), jnp.bfloat16), pltpu.VMEM((HD, tokens), jnp.bfloat16)],
        ),
        compiler_params=pltpu.CompilerParams(
            dimension_semantics=("arbitrary",), vmem_limit_bytes=48 * 1024 * 1024
        ),
    )(share, got, got, got, gain_q.reshape(1, HD), gain_k.reshape(1, HD))


def _pack_kernel(q_ref, k_ref, v_ref, o_ref):
    group = q_ref.shape[1] // HD
    copies = o_ref.shape[0] // group
    for i in range(group):
        for c in range(copies):
            for j, ref in enumerate((q_ref, k_ref, v_ref)):
                o_ref[i * copies + c, j] = ref[:, i * HD:(i + 1) * HD]


def pack(queries, keys, values, copies):
    rows = queries.shape[0]
    group = 8
    spec = pl.BlockSpec((rows, group * HD), lambda g: (0, g))
    return pl.pallas_call(
        _pack_kernel,
        out_shape=jax.ShapeDtypeStruct((HEADS * copies, 3, rows, HD), jnp.bfloat16),
        grid=(HEADS // group,),
        in_specs=[spec, spec, spec],
        out_specs=pl.BlockSpec((group * copies, 3, rows, HD), lambda g: (g, 0, 0, 0)),
    )(queries, keys, values)


def body(queries, keys, values, gain_q, gain_k, w_latent, w_temporal, w_decode):
    devices = lax.axis_size("seq")
    copies = devices // HEADS
    rows = queries.shape[0]

    stacked = pack(queries, keys, values, copies)
    got = lax.all_to_all(stacked, "seq", split_axis=0, concat_axis=0, tiled=True)
    share = lax.axis_index("seq") % copies
    span_blocks = devices // copies
    out = attend(got, jnp.reshape(share, (1,)).astype(jnp.int32), span_blocks, gain_q, gain_k)
    if copies > 1:
        placed = jnp.zeros((copies, span_blocks, rows, HD), jnp.bfloat16)
        placed = lax.dynamic_update_index_in_dim(placed, out, share, 0)
        out = placed.reshape(devices, rows, HD)
    back = lax.all_to_all(out, "seq", split_axis=0, concat_axis=0, tiled=True)
    if copies > 1:
        back = jnp.sum(back.reshape(HEADS, copies, rows, HD).astype(jnp.float32), axis=1)
        back = back.astype(jnp.bfloat16)
    back = back.reshape(HEADS, rows, HD)
    latent = jnp.einsum(
        "hrd,hdc->rc", back, w_latent.reshape(HEADS, HD, -1), preferred_element_type=jnp.float32
    ).astype(jnp.bfloat16)
    attention = jnp.transpose(back, (1, 0, 2)).reshape(rows, HEADS * HD)
    peers = lax.axis_size("seq")
    odd = lax.axis_index("seq") % 2 == 1
    partner = lax.ppermute(latent, "seq", [(i, i ^ 1) for i in range(peers)])
    pair = jnp.stack([jnp.where(odd, partner, latent), jnp.where(odd, latent, partner)])
    prior = passed_along(pair, "seq", 2)
    earlier_one = jnp.where(odd, partner, prior[1])
    earlier_two = jnp.where(odd, prior[1], prior[0])
    taps = jnp.concatenate([latent, earlier_one, earlier_two], axis=1)
    state = jnp.dot(taps, w_temporal.reshape(-1, w_temporal.shape[2]), preferred_element_type=jnp.float32)
    act = lax.optimization_barrier(jax.nn.silu(state).astype(jnp.bfloat16))
    decoded = jnp.dot(act, w_decode, preferred_element_type=jnp.float32).astype(jnp.bfloat16)
    return (attention, decoded)


def solution(mesh):
    in_specs = (
        P(("groups", "seq"), None),
        P(("groups", "seq"), None),
        P(("groups", "seq"), None),
        P(),
        P(),
        P(),
        P(),
        P(),
    )
    out_specs = (P(("groups", "seq"), None), P(("groups", "seq"), None))
    return jax.shard_map(body, mesh=mesh, in_specs=in_specs, out_specs=out_specs, check_vma=False)
```

```python
import math

import jax
import jax.numpy as jnp
from jax import lax
from jax.experimental import pallas as pl
from jax.experimental.pallas import tpu as pltpu
from jax.sharding import PartitionSpec as P

HEADS = 16
HD = 128
EPS = 1e-06


def passed_along(shard, axis, by):
    peers = lax.axis_size(axis)
    pairs = [(i, i + by) for i in range(peers) if 0 <= i + by < peers]
    return lax.ppermute(shard, axis, pairs)


def _norm(x, gain):
    x = x.astype(jnp.float32)
    x = x * lax.rsqrt(jnp.mean(x * x, axis=-1, keepdims=True) + EPS) * gain
    return x.astype(jnp.bfloat16)


def _attn_kernel(share_ref, q_ref, k_ref, v_ref, gq_ref, gk_ref, o_ref, kn_ref, vt_ref):
    @pl.when(pl.program_id(0) == 0)
    def _():
        k = k_ref[...]
        k = k.reshape(k.shape[0] * k.shape[1], HD)
        kn_ref[...] = _norm(k, gk_ref[...])
        v = v_ref[...]
        vt_ref[...] = v.reshape(v.shape[0] * v.shape[1], HD).T

    q = q_ref[...]
    q = q.reshape(q.shape[0] * q.shape[1], HD)
    qt = _norm(q, gq_ref[...]).T
    st = jnp.dot(kn_ref[...], qt, preferred_element_type=jnp.float32)
    c = math.log2(math.e) / math.sqrt(HD)
    m = jnp.max(st, axis=0, keepdims=True)
    e = jnp.exp2(st * c - m * c)
    total = jnp.sum(e, axis=0, keepdims=True)
    out_t = jnp.dot(vt_ref[...], e.astype(jnp.bfloat16), preferred_element_type=jnp.float32)
    out = (out_t / total).T.astype(jnp.bfloat16)
    o_ref[...] = out.reshape(o_ref.shape)


def attend(got, share, span_blocks, gain_q, gain_k):
    src, _, rows, _ = got.shape
    tokens = src * rows
    qb = max(1, min(span_blocks, (4 << 20) // (tokens * rows)))
    steps = span_blocks // qb
    tokens = src * rows
    return pl.pallas_call(
        _attn_kernel,
        out_shape=jax.ShapeDtypeStruct((span_blocks, rows, HD), jnp.bfloat16),
        grid_spec=pltpu.PrefetchScalarGridSpec(
            num_scalar_prefetch=1,
            grid=(steps,),
            in_specs=[
                pl.BlockSpec((qb, None, rows, HD), lambda i, sh: (sh[0] * steps + i, 0, 0, 0)),
                pl.BlockSpec((src, None, rows, HD), lambda i, sh: (0, 1, 0, 0)),
                pl.BlockSpec((src, None, rows, HD), lambda i, sh: (0, 2, 0, 0)),
                pl.BlockSpec((1, HD), lambda i, sh: (0, 0)),
                pl.BlockSpec((1, HD), lambda i, sh: (0, 0)),
            ],
            out_specs=pl.BlockSpec((qb, rows, HD), lambda i, sh: (i, 0, 0)),
            scratch_shapes=[pltpu.VMEM((tokens, HD), jnp.bfloat16), pltpu.VMEM((HD, tokens), jnp.bfloat16)],
        ),
        compiler_params=pltpu.CompilerParams(
            dimension_semantics=("arbitrary",), vmem_limit_bytes=48 * 1024 * 1024
        ),
    )(share, got, got, got, gain_q.reshape(1, HD), gain_k.reshape(1, HD))


def _pack_kernel(q_ref, k_ref, v_ref, o_ref):
    group = q_ref.shape[1] // HD
    copies = o_ref.shape[0] // group
    for i in range(group):
        for c in range(copies):
            for j, ref in enumerate((q_ref, k_ref, v_ref)):
                o_ref[i * copies + c, j] = ref[:, i * HD:(i + 1) * HD]


def pack(queries, keys, values, copies):
    rows = queries.shape[0]
    group = 8
    spec = pl.BlockSpec((rows, group * HD), lambda g: (0, g))
    return pl.pallas_call(
        _pack_kernel,
        out_shape=jax.ShapeDtypeStruct((HEADS * copies, 3, rows, HD), jnp.bfloat16),
        grid=(HEADS // group,),
        in_specs=[spec, spec, spec],
        out_specs=pl.BlockSpec((group * copies, 3, rows, HD), lambda g: (g, 0, 0, 0)),
    )(queries, keys, values)


def body(queries, keys, values, gain_q, gain_k, w_latent, w_temporal, w_decode):
    devices = lax.axis_size("seq")
    copies = devices // HEADS
    rows = queries.shape[0]

    stacked = pack(queries, keys, values, copies)
    got = lax.all_to_all(stacked, "seq", split_axis=0, concat_axis=0, tiled=True)
    share = lax.axis_index("seq") % copies
    span_blocks = devices // copies
    out = attend(got, jnp.reshape(share, (1,)).astype(jnp.int32), span_blocks, gain_q, gain_k)
    if copies > 1:
        placed = jnp.zeros((copies, span_blocks, rows, HD), jnp.bfloat16)
        placed = lax.dynamic_update_index_in_dim(placed, out, share, 0)
        out = placed.reshape(devices, rows, HD)
    back = lax.all_to_all(out, "seq", split_axis=0, concat_axis=0, tiled=True)
    if copies > 1:
        back = jnp.sum(back.reshape(HEADS, copies, rows, HD).astype(jnp.float32), axis=1)
        back = back.astype(jnp.bfloat16)
    back = back.reshape(HEADS, rows, HD)
    latent = jnp.einsum(
        "hrd,hdc->rc", back, w_latent.reshape(HEADS, HD, -1), preferred_element_type=jnp.float32
    ).astype(jnp.bfloat16)
    attention = jnp.transpose(back, (1, 0, 2)).reshape(rows, HEADS * HD)
    earlier_one = passed_along(latent, "seq", 1)
    earlier_two = passed_along(latent, "seq", 2)
    state = jnp.dot(latent, w_temporal[0], preferred_element_type=jnp.float32)
    state = state + jnp.dot(earlier_one, w_temporal[1], preferred_element_type=jnp.float32)
    state = state + jnp.dot(earlier_two, w_temporal[2], preferred_element_type=jnp.float32)
    act = jax.nn.silu(state).astype(jnp.bfloat16)
    decoded = jnp.dot(act, w_decode, preferred_element_type=jnp.float32).astype(jnp.bfloat16)
    return (attention, decoded)


def solution(mesh):
    in_specs = (
        P(("groups", "seq"), None),
        P(("groups", "seq"), None),
        P(("groups", "seq"), None),
        P(),
        P(),
        P(),
        P(),
        P(),
    )
    out_specs = (P(("groups", "seq"), None), P(("groups", "seq"), None))
    return jax.shard_map(body, mesh=mesh, in_specs=in_specs, out_specs=out_specs, check_vma=False)
```

```python
import math

import jax
import jax.numpy as jnp
from jax import lax
from jax.experimental import pallas as pl
from jax.experimental.pallas import tpu as pltpu
from jax.sharding import PartitionSpec as P

HEADS = 16
HD = 128
EPS = 1e-06


def passed_along(shard, axis, by):
    peers = lax.axis_size(axis)
    pairs = [(i, i + by) for i in range(peers) if 0 <= i + by < peers]
    return lax.ppermute(shard, axis, pairs)


def _norm(x, gain):
    x = x.astype(jnp.float32)
    x = x * lax.rsqrt(jnp.mean(x * x, axis=-1, keepdims=True) + EPS) * gain
    return x.astype(jnp.bfloat16)


def _attn_kernel(share_ref, q_ref, k_ref, v_ref, gq_ref, gk_ref, o_ref, kn_ref, vt_ref):
    @pl.when(pl.program_id(0) == 0)
    def _():
        k = k_ref[...]
        k = k.reshape(k.shape[0] * k.shape[1], HD)
        kn_ref[...] = _norm(k, gk_ref[...])
        v = v_ref[...]
        vt_ref[...] = v.reshape(v.shape[0] * v.shape[1], HD).T

    q = q_ref[...]
    q = q.reshape(q.shape[0] * q.shape[1], HD)
    qt = _norm(q, gq_ref[...]).T
    st = jnp.dot(kn_ref[...], qt, preferred_element_type=jnp.float32)
    c = math.log2(math.e) / math.sqrt(HD)
    m = jnp.max(st, axis=0, keepdims=True)
    e = jnp.exp2(st * c - m * c)
    total = jnp.sum(e, axis=0, keepdims=True)
    out_t = jnp.dot(vt_ref[...], e.astype(jnp.bfloat16), preferred_element_type=jnp.float32)
    out = (out_t / total).T.astype(jnp.bfloat16)
    o_ref[...] = out.reshape(o_ref.shape)


def attend(got, share, span_blocks, gain_q, gain_k):
    src, _, rows, _ = got.shape
    tokens = src * rows
    qb = max(1, min(span_blocks, (4 << 20) // (tokens * rows)))
    steps = span_blocks // qb
    tokens = src * rows
    return pl.pallas_call(
        _attn_kernel,
        out_shape=jax.ShapeDtypeStruct((span_blocks, rows, HD), jnp.bfloat16),
        grid_spec=pltpu.PrefetchScalarGridSpec(
            num_scalar_prefetch=1,
            grid=(steps,),
            in_specs=[
                pl.BlockSpec((qb, None, rows, HD), lambda i, sh: (sh[0] * steps + i, 0, 0, 0)),
                pl.BlockSpec((src, None, rows, HD), lambda i, sh: (0, 1, 0, 0)),
                pl.BlockSpec((src, None, rows, HD), lambda i, sh: (0, 2, 0, 0)),
                pl.BlockSpec((1, HD), lambda i, sh: (0, 0)),
                pl.BlockSpec((1, HD), lambda i, sh: (0, 0)),
            ],
            out_specs=pl.BlockSpec((qb, rows, HD), lambda i, sh: (i, 0, 0)),
            scratch_shapes=[pltpu.VMEM((tokens, HD), jnp.bfloat16), pltpu.VMEM((HD, tokens), jnp.bfloat16)],
        ),
        compiler_params=pltpu.CompilerParams(
            dimension_semantics=("arbitrary",), vmem_limit_bytes=48 * 1024 * 1024
        ),
    )(share, got, got, got, gain_q.reshape(1, HD), gain_k.reshape(1, HD))


def _pack_kernel(q_ref, k_ref, v_ref, o_ref):
    group = q_ref.shape[1] // HD
    copies = o_ref.shape[0] // group
    for i in range(group):
        for c in range(copies):
            for j, ref in enumerate((q_ref, k_ref, v_ref)):
                o_ref[i * copies + c, j] = ref[:, i * HD:(i + 1) * HD]


def pack(queries, keys, values, copies):
    rows = queries.shape[0]
    group = 8
    spec = pl.BlockSpec((rows, group * HD), lambda g: (0, g))
    return pl.pallas_call(
        _pack_kernel,
        out_shape=jax.ShapeDtypeStruct((HEADS * copies, 3, rows, HD), jnp.bfloat16),
        grid=(HEADS // group,),
        in_specs=[spec, spec, spec],
        out_specs=pl.BlockSpec((group * copies, 3, rows, HD), lambda g: (g, 0, 0, 0)),
    )(queries, keys, values)


def body(queries, keys, values, gain_q, gain_k, w_latent, w_temporal, w_decode):
    devices = lax.axis_size("seq")
    copies = devices // HEADS
    rows = queries.shape[0]

    stacked = pack(queries, keys, values, copies)
    got = lax.all_to_all(stacked, "seq", split_axis=0, concat_axis=0, tiled=True)
    share = lax.axis_index("seq") % copies
    span_blocks = devices // copies
    out = attend(got, jnp.reshape(share, (1,)).astype(jnp.int32), span_blocks, gain_q, gain_k)
    if copies > 1:
        placed = jnp.zeros((copies, span_blocks, rows, HD), jnp.bfloat16)
        placed = lax.dynamic_update_index_in_dim(placed, out, share, 0)
        out = placed.reshape(devices, rows, HD)
    back = lax.all_to_all(out, "seq", split_axis=0, concat_axis=0, tiled=True)
    if copies > 1:
        back = jnp.sum(back.reshape(HEADS, copies, rows, HD).astype(jnp.float32), axis=1)
        back = back.astype(jnp.bfloat16)
    back = back.reshape(HEADS, rows, HD)
    latent = jnp.einsum(
        "hrd,hdc->rc", back, w_latent.reshape(HEADS, HD, -1), preferred_element_type=jnp.float32
    ).astype(jnp.bfloat16)
    attention = jnp.transpose(back, (1, 0, 2)).reshape(rows, HEADS * HD)
    earlier_one = passed_along(latent, "seq", 1)
    earlier_two = passed_along(latent, "seq", 2)
    taps = jnp.concatenate([latent, earlier_one, earlier_two], axis=1)
    state = jnp.dot(taps, w_temporal.reshape(-1, w_temporal.shape[2]), preferred_element_type=jnp.float32)
    act = jax.nn.silu(state).astype(jnp.bfloat16)
    decoded = jnp.dot(act, w_decode, preferred_element_type=jnp.float32).astype(jnp.bfloat16)
    return (attention, decoded)


def solution(mesh):
    in_specs = (
        P(("groups", "seq"), None),
        P(("groups", "seq"), None),
        P(("groups", "seq"), None),
        P(),
        P(),
        P(),
        P(),
        P(),
    )
    out_specs = (P(("groups", "seq"), None), P(("groups", "seq"), None))
    return jax.shard_map(body, mesh=mesh, in_specs=in_specs, out_specs=out_specs, check_vma=False)
```

```python
import math

import jax
import jax.numpy as jnp
from jax import lax
from jax.experimental import pallas as pl
from jax.experimental.pallas import tpu as pltpu
from jax.sharding import PartitionSpec as P

HEADS = 16
HD = 128
EPS = 1e-06


def passed_along(shard, axis, by):
    peers = lax.axis_size(axis)
    pairs = [(i, i + by) for i in range(peers) if 0 <= i + by < peers]
    return lax.ppermute(shard, axis, pairs)


def _norm(x, gain):
    x = x.astype(jnp.float32)
    x = x * lax.rsqrt(jnp.mean(x * x, axis=-1, keepdims=True) + EPS) * gain
    return x.astype(jnp.bfloat16)


def _attn_kernel(share_ref, q_ref, k_ref, v_ref, gq_ref, gk_ref, o_ref, kn_ref, vt_ref):
    @pl.when(pl.program_id(0) == 0)
    def _():
        k = k_ref[...]
        k = k.reshape(k.shape[0] * k.shape[1], HD)
        kn_ref[...] = _norm(k, gk_ref[...])
        v = v_ref[...]
        vt_ref[...] = v.reshape(v.shape[0] * v.shape[1], HD).T

    q = q_ref[...]
    q = q.reshape(q.shape[0] * q.shape[1], HD)
    qt = _norm(q, gq_ref[...]).T
    st = jnp.dot(kn_ref[...], qt, preferred_element_type=jnp.float32)
    c = math.log2(math.e) / math.sqrt(HD)
    m = jnp.max(st, axis=0, keepdims=True)
    e = jnp.exp2((st - m) * c)
    total = jnp.sum(e, axis=0, keepdims=True)
    out_t = jnp.dot(vt_ref[...], e.astype(jnp.bfloat16), preferred_element_type=jnp.float32)
    out = (out_t / total).T.astype(jnp.bfloat16)
    o_ref[...] = out.reshape(o_ref.shape)


def attend(got, share, span_blocks, gain_q, gain_k):
    src, _, rows, _ = got.shape
    tokens = src * rows
    qb = max(1, min(span_blocks, (4 << 20) // (tokens * rows)))
    steps = span_blocks // qb
    tokens = src * rows
    return pl.pallas_call(
        _attn_kernel,
        out_shape=jax.ShapeDtypeStruct((span_blocks, rows, HD), jnp.bfloat16),
        grid_spec=pltpu.PrefetchScalarGridSpec(
            num_scalar_prefetch=1,
            grid=(steps,),
            in_specs=[
                pl.BlockSpec((qb, None, rows, HD), lambda i, sh: (sh[0] * steps + i, 0, 0, 0)),
                pl.BlockSpec((src, None, rows, HD), lambda i, sh: (0, 1, 0, 0)),
                pl.BlockSpec((src, None, rows, HD), lambda i, sh: (0, 2, 0, 0)),
                pl.BlockSpec((1, HD), lambda i, sh: (0, 0)),
                pl.BlockSpec((1, HD), lambda i, sh: (0, 0)),
            ],
            out_specs=pl.BlockSpec((qb, rows, HD), lambda i, sh: (i, 0, 0)),
            scratch_shapes=[pltpu.VMEM((tokens, HD), jnp.bfloat16), pltpu.VMEM((HD, tokens), jnp.bfloat16)],
        ),
        compiler_params=pltpu.CompilerParams(
            dimension_semantics=("arbitrary",), vmem_limit_bytes=48 * 1024 * 1024
        ),
    )(share, got, got, got, gain_q.reshape(1, HD), gain_k.reshape(1, HD))


def _pack_kernel(q_ref, k_ref, v_ref, o_ref):
    group = q_ref.shape[1] // HD
    copies = o_ref.shape[0] // group
    for i in range(group):
        for c in range(copies):
            for j, ref in enumerate((q_ref, k_ref, v_ref)):
                o_ref[i * copies + c, j] = ref[:, i * HD:(i + 1) * HD]


def pack(queries, keys, values, copies):
    rows = queries.shape[0]
    group = 8
    spec = pl.BlockSpec((rows, group * HD), lambda g: (0, g))
    return pl.pallas_call(
        _pack_kernel,
        out_shape=jax.ShapeDtypeStruct((HEADS * copies, 3, rows, HD), jnp.bfloat16),
        grid=(HEADS // group,),
        in_specs=[spec, spec, spec],
        out_specs=pl.BlockSpec((group * copies, 3, rows, HD), lambda g: (g, 0, 0, 0)),
    )(queries, keys, values)


def body(queries, keys, values, gain_q, gain_k, w_latent, w_temporal, w_decode):
    devices = lax.axis_size("seq")
    copies = devices // HEADS
    rows = queries.shape[0]

    stacked = pack(queries, keys, values, copies)
    got = lax.all_to_all(stacked, "seq", split_axis=0, concat_axis=0, tiled=True)
    share = lax.axis_index("seq") % copies
    span_blocks = devices // copies
    out = attend(got, jnp.reshape(share, (1,)).astype(jnp.int32), span_blocks, gain_q, gain_k)
    if copies > 1:
        placed = jnp.zeros((copies, span_blocks, rows, HD), jnp.bfloat16)
        placed = lax.dynamic_update_index_in_dim(placed, out, share, 0)
        out = placed.reshape(devices, rows, HD)
    back = lax.all_to_all(out, "seq", split_axis=0, concat_axis=0, tiled=True)
    if copies > 1:
        back = jnp.sum(back.reshape(HEADS, copies, rows, HD).astype(jnp.float32), axis=1)
        back = back.astype(jnp.bfloat16)
    back = back.reshape(HEADS, rows, HD)
    latent = jnp.einsum(
        "hrd,hdc->rc", back, w_latent.reshape(HEADS, HD, -1), preferred_element_type=jnp.float32
    ).astype(jnp.bfloat16)
    attention = jnp.transpose(back, (1, 0, 2)).reshape(rows, HEADS * HD)
    earlier_one = passed_along(latent, "seq", 1)
    earlier_two = passed_along(latent, "seq", 2)
    taps = jnp.concatenate([latent, earlier_one, earlier_two], axis=1)
    state = jnp.dot(taps, w_temporal.reshape(-1, w_temporal.shape[2]), preferred_element_type=jnp.float32)
    act = lax.optimization_barrier(jax.nn.silu(state).astype(jnp.bfloat16))
    decoded = jnp.dot(act, w_decode, preferred_element_type=jnp.float32).astype(jnp.bfloat16)
    return (attention, decoded)


def solution(mesh):
    in_specs = (
        P(("groups", "seq"), None),
        P(("groups", "seq"), None),
        P(("groups", "seq"), None),
        P(),
        P(),
        P(),
        P(),
        P(),
    )
    out_specs = (P(("groups", "seq"), None), P(("groups", "seq"), None))
    return jax.shard_map(body, mesh=mesh, in_specs=in_specs, out_specs=out_specs, check_vma=False)
```

```python
import math

import jax
import jax.numpy as jnp
from jax import lax
from jax.experimental import pallas as pl
from jax.experimental.pallas import tpu as pltpu
from jax.sharding import PartitionSpec as P

HEADS = 16
HD = 128
EPS = 1e-06


def passed_along(shard, axis, by):
    peers = lax.axis_size(axis)
    pairs = [(i, i + by) for i in range(peers) if 0 <= i + by < peers]
    return lax.ppermute(shard, axis, pairs)


def _norm(x, gain):
    x = x.astype(jnp.float32)
    x = x * lax.rsqrt(jnp.mean(x * x, axis=-1, keepdims=True) + EPS) * gain
    return x.astype(jnp.bfloat16)


def _attn_kernel(share_ref, q_ref, k_ref, v_ref, gq_ref, gk_ref, o_ref, kn_ref, vt_ref):
    @pl.when(pl.program_id(0) == 0)
    def _():
        k = k_ref[...]
        k = k.reshape(k.shape[0] * k.shape[1], HD)
        kn_ref[...] = _norm(k, gk_ref[...])
        v = v_ref[...]
        vt_ref[...] = v.reshape(v.shape[0] * v.shape[1], HD).T

    q = q_ref[...]
    q = q.reshape(q.shape[0] * q.shape[1], HD)
    qt = q.T.astype(jnp.float32)
    qt = qt * lax.rsqrt(jnp.mean(qt * qt, axis=0, keepdims=True) + EPS) * gq_ref[...].T
    qt = qt.astype(jnp.bfloat16)
    st = jnp.dot(kn_ref[...], qt, preferred_element_type=jnp.float32)
    c = math.log2(math.e) / math.sqrt(HD)
    m = jnp.max(st, axis=0, keepdims=True)
    e = jnp.exp2((st - m) * c)
    total = jnp.sum(e, axis=0, keepdims=True)
    out_t = jnp.dot(vt_ref[...], e.astype(jnp.bfloat16), preferred_element_type=jnp.float32)
    out = (out_t / total).T.astype(jnp.bfloat16)
    o_ref[...] = out.reshape(o_ref.shape)


def attend(got, share, span_blocks, gain_q, gain_k):
    src, _, rows, _ = got.shape
    tokens = src * rows
    qb = max(1, min(span_blocks, (4 << 20) // (tokens * rows)))
    steps = span_blocks // qb
    tokens = src * rows
    return pl.pallas_call(
        _attn_kernel,
        out_shape=jax.ShapeDtypeStruct((span_blocks, rows, HD), jnp.bfloat16),
        grid_spec=pltpu.PrefetchScalarGridSpec(
            num_scalar_prefetch=1,
            grid=(steps,),
            in_specs=[
                pl.BlockSpec((qb, None, rows, HD), lambda i, sh: (sh[0] * steps + i, 0, 0, 0)),
                pl.BlockSpec((src, None, rows, HD), lambda i, sh: (0, 1, 0, 0)),
                pl.BlockSpec((src, None, rows, HD), lambda i, sh: (0, 2, 0, 0)),
                pl.BlockSpec((1, HD), lambda i, sh: (0, 0)),
                pl.BlockSpec((1, HD), lambda i, sh: (0, 0)),
            ],
            out_specs=pl.BlockSpec((qb, rows, HD), lambda i, sh: (i, 0, 0)),
            scratch_shapes=[pltpu.VMEM((tokens, HD), jnp.bfloat16), pltpu.VMEM((HD, tokens), jnp.bfloat16)],
        ),
        compiler_params=pltpu.CompilerParams(
            dimension_semantics=("arbitrary",), vmem_limit_bytes=48 * 1024 * 1024
        ),
    )(share, got, got, got, gain_q.reshape(1, HD), gain_k.reshape(1, HD))


def _pack_kernel(q_ref, k_ref, v_ref, o_ref):
    group = q_ref.shape[1] // HD
    copies = o_ref.shape[0] // group
    for i in range(group):
        for c in range(copies):
            for j, ref in enumerate((q_ref, k_ref, v_ref)):
                o_ref[i * copies + c, j] = ref[:, i * HD:(i + 1) * HD]


def pack(queries, keys, values, copies):
    rows = queries.shape[0]
    group = 8
    spec = pl.BlockSpec((rows, group * HD), lambda g: (0, g))
    return pl.pallas_call(
        _pack_kernel,
        out_shape=jax.ShapeDtypeStruct((HEADS * copies, 3, rows, HD), jnp.bfloat16),
        grid=(HEADS // group,),
        in_specs=[spec, spec, spec],
        out_specs=pl.BlockSpec((group * copies, 3, rows, HD), lambda g: (g, 0, 0, 0)),
    )(queries, keys, values)


def body(queries, keys, values, gain_q, gain_k, w_latent, w_temporal, w_decode):
    devices = lax.axis_size("seq")
    copies = devices // HEADS
    rows = queries.shape[0]

    stacked = pack(queries, keys, values, copies)
    got = lax.all_to_all(stacked, "seq", split_axis=0, concat_axis=0, tiled=True)
    share = lax.axis_index("seq") % copies
    span_blocks = devices // copies
    out = attend(got, jnp.reshape(share, (1,)).astype(jnp.int32), span_blocks, gain_q, gain_k)
    if copies > 1:
        placed = jnp.zeros((copies, span_blocks, rows, HD), jnp.bfloat16)
        placed = lax.dynamic_update_index_in_dim(placed, out, share, 0)
        out = placed.reshape(devices, rows, HD)
    back = lax.all_to_all(out, "seq", split_axis=0, concat_axis=0, tiled=True)
    if copies > 1:
        back = jnp.sum(back.reshape(HEADS, copies, rows, HD).astype(jnp.float32), axis=1)
        back = back.astype(jnp.bfloat16)
    back = back.reshape(HEADS, rows, HD)
    latent = jnp.einsum(
        "hrd,hdc->rc", back, w_latent.reshape(HEADS, HD, -1), preferred_element_type=jnp.float32
    ).astype(jnp.bfloat16)
    attention = jnp.transpose(back, (1, 0, 2)).reshape(rows, HEADS * HD)
    earlier_one = passed_along(latent, "seq", 1)
    earlier_two = passed_along(latent, "seq", 2)
    taps = jnp.concatenate([latent, earlier_one, earlier_two], axis=1)
    state = jnp.dot(taps, w_temporal.reshape(-1, w_temporal.shape[2]), preferred_element_type=jnp.float32)
    act = lax.optimization_barrier(jax.nn.silu(state).astype(jnp.bfloat16))
    decoded = jnp.dot(act, w_decode, preferred_element_type=jnp.float32).astype(jnp.bfloat16)
    return (attention, decoded)


def solution(mesh):
    in_specs = (
        P(("groups", "seq"), None),
        P(("groups", "seq"), None),
        P(("groups", "seq"), None),
        P(),
        P(),
        P(),
        P(),
        P(),
    )
    out_specs = (P(("groups", "seq"), None), P(("groups", "seq"), None))
    return jax.shard_map(body, mesh=mesh, in_specs=in_specs, out_specs=out_specs, check_vma=False)
```

```python
import math

import jax
import jax.numpy as jnp
from jax import lax
from jax.experimental import pallas as pl
from jax.experimental.pallas import tpu as pltpu
from jax.sharding import PartitionSpec as P

HEADS = 16
HD = 128
EPS = 1e-06


def passed_along(shard, axis, by):
    peers = lax.axis_size(axis)
    pairs = [(i, i + by) for i in range(peers) if 0 <= i + by < peers]
    return lax.ppermute(shard, axis, pairs)


def _norm(x, gain):
    x = x.astype(jnp.float32)
    x = x * lax.rsqrt(jnp.mean(x * x, axis=-1, keepdims=True) + EPS) * gain
    return x.astype(jnp.bfloat16)


def _attn_kernel(share_ref, q_ref, k_ref, v_ref, gq_ref, gk_ref, o_ref, kn_ref, vt_ref):
    @pl.when(pl.program_id(0) == 0)
    def _():
        k = k_ref[...]
        k = k.reshape(k.shape[0] * k.shape[1], HD)
        kn_ref[...] = _norm(k, gk_ref[...])
        v = v_ref[...]
        vt_ref[...] = v.reshape(v.shape[0] * v.shape[1], HD).T

    q = q_ref[...]
    q = q.reshape(q.shape[0] * q.shape[1], HD)
    qt = q.T.astype(jnp.float32)
    qt = qt * lax.rsqrt(jnp.mean(qt * qt, axis=0, keepdims=True) + EPS) * gq_ref[...].T
    qt = qt.astype(jnp.bfloat16)
    st = jnp.dot(kn_ref[...], qt, preferred_element_type=jnp.float32)
    c = math.log2(math.e) / math.sqrt(HD)
    m = jnp.max(st, axis=0, keepdims=True)
    e = jnp.exp2((st - m) * c)
    total = jnp.sum(e, axis=0, keepdims=True)
    out_t = jnp.dot(vt_ref[...], e.astype(jnp.bfloat16), preferred_element_type=jnp.float32)
    out = (out_t / total).T.astype(jnp.bfloat16)
    o_ref[...] = out.reshape(o_ref.shape)


def attend(got, share, span_blocks, gain_q, gain_k):
    src, _, rows, _ = got.shape
    tokens = src * rows
    qb = max(1, min(span_blocks, (4 << 20) // (tokens * rows)))
    steps = span_blocks // qb
    tokens = src * rows
    return pl.pallas_call(
        _attn_kernel,
        out_shape=jax.ShapeDtypeStruct((span_blocks, rows, HD), jnp.bfloat16),
        grid_spec=pltpu.PrefetchScalarGridSpec(
            num_scalar_prefetch=1,
            grid=(steps,),
            in_specs=[
                pl.BlockSpec((qb, None, rows, HD), lambda i, sh: (sh[0] * steps + i, 0, 0, 0)),
                pl.BlockSpec((src, None, rows, HD), lambda i, sh: (0, 1, 0, 0)),
                pl.BlockSpec((src, None, rows, HD), lambda i, sh: (0, 2, 0, 0)),
                pl.BlockSpec((1, HD), lambda i, sh: (0, 0)),
                pl.BlockSpec((1, HD), lambda i, sh: (0, 0)),
            ],
            out_specs=pl.BlockSpec((qb, rows, HD), lambda i, sh: (i, 0, 0)),
            scratch_shapes=[pltpu.VMEM((tokens, HD), jnp.bfloat16), pltpu.VMEM((HD, tokens), jnp.bfloat16)],
        ),
        compiler_params=pltpu.CompilerParams(
            dimension_semantics=("arbitrary",), vmem_limit_bytes=48 * 1024 * 1024
        ),
    )(share, got, got, got, gain_q.reshape(1, HD), gain_k.reshape(1, HD))


def _pack_kernel(q_ref, k_ref, v_ref, o_ref):
    group = q_ref.shape[1] // HD
    copies = o_ref.shape[0] // group
    for i in range(group):
        for c in range(copies):
            for j, ref in enumerate((q_ref, k_ref, v_ref)):
                o_ref[i * copies + c, j] = ref[:, i * HD:(i + 1) * HD]


def pack(queries, keys, values, copies):
    rows = queries.shape[0]
    group = 8
    spec = pl.BlockSpec((rows, group * HD), lambda g: (0, g))
    return pl.pallas_call(
        _pack_kernel,
        out_shape=jax.ShapeDtypeStruct((HEADS * copies, 3, rows, HD), jnp.bfloat16),
        grid=(HEADS // group,),
        in_specs=[spec, spec, spec],
        out_specs=pl.BlockSpec((group * copies, 3, rows, HD), lambda g: (g, 0, 0, 0)),
    )(queries, keys, values)


def body(queries, keys, values, gain_q, gain_k, w_latent, w_temporal, w_decode):
    devices = lax.axis_size("seq")
    copies = devices // HEADS
    rows = queries.shape[0]

    stacked = pack(queries, keys, values, copies)
    got = lax.all_to_all(stacked, "seq", split_axis=0, concat_axis=0, tiled=True)
    share = lax.axis_index("seq") % copies
    span_blocks = devices // copies
    out = attend(got, jnp.reshape(share, (1,)).astype(jnp.int32), span_blocks, gain_q, gain_k)
    if copies > 1:
        placed = jnp.zeros((copies, span_blocks, rows, HD), jnp.bfloat16)
        placed = lax.dynamic_update_index_in_dim(placed, out, share, 0)
        out = placed.reshape(devices, rows, HD)
    back = lax.all_to_all(out, "seq", split_axis=0, concat_axis=0, tiled=True)
    if copies > 1:
        back = jnp.sum(back.reshape(HEADS, copies, rows, HD).astype(jnp.float32), axis=1)
        back = back.astype(jnp.bfloat16)
    back = back.reshape(HEADS, rows, HD)
    latent = jnp.einsum(
        "hrd,hdc->rc", back, w_latent.reshape(HEADS, HD, -1), preferred_element_type=jnp.float32
    ).astype(jnp.bfloat16)
    attention = jnp.concatenate([back[h] for h in range(HEADS)], axis=1)
    earlier_one = passed_along(latent, "seq", 1)
    earlier_two = passed_along(latent, "seq", 2)
    taps = jnp.concatenate([latent, earlier_one, earlier_two], axis=1)
    state = jnp.dot(taps, w_temporal.reshape(-1, w_temporal.shape[2]), preferred_element_type=jnp.float32)
    act = lax.optimization_barrier(jax.nn.silu(state).astype(jnp.bfloat16))
    decoded = jnp.dot(act, w_decode, preferred_element_type=jnp.float32).astype(jnp.bfloat16)
    return (attention, decoded)


def solution(mesh):
    in_specs = (
        P(("groups", "seq"), None),
        P(("groups", "seq"), None),
        P(("groups", "seq"), None),
        P(),
        P(),
        P(),
        P(),
        P(),
    )
    out_specs = (P(("groups", "seq"), None), P(("groups", "seq"), None))
    return jax.shard_map(body, mesh=mesh, in_specs=in_specs, out_specs=out_specs, check_vma=False)
```

```python
import math

import jax
import jax.numpy as jnp
from jax import lax
from jax.experimental import pallas as pl
from jax.experimental.pallas import tpu as pltpu
from jax.sharding import PartitionSpec as P

HEADS = 16
HD = 128
EPS = 1e-06


def passed_along(shard, axis, by):
    peers = lax.axis_size(axis)
    pairs = [(i, i + by) for i in range(peers) if 0 <= i + by < peers]
    return lax.ppermute(shard, axis, pairs)


def _norm(x, gain):
    x = x.astype(jnp.float32)
    x = x * lax.rsqrt(jnp.mean(x * x, axis=-1, keepdims=True) + EPS) * gain
    return x.astype(jnp.bfloat16)


def _attn_kernel(share_ref, q_ref, k_ref, v_ref, gq_ref, gk_ref, o_ref, kn_ref, vt_ref):
    @pl.when(pl.program_id(0) == 0)
    def _():
        k = k_ref[...]
        k = k.reshape(k.shape[0] * k.shape[1], HD)
        kn_ref[...] = _norm(k, gk_ref[...])
        v = v_ref[...]
        vt_ref[...] = v.reshape(v.shape[0] * v.shape[1], HD).T

    q = q_ref[...]
    q = q.reshape(q.shape[0] * q.shape[1], HD)
    qt = q.T.astype(jnp.float32)
    qt = qt * lax.rsqrt(jnp.mean(qt * qt, axis=0, keepdims=True) + EPS) * gq_ref[...].T
    qt = qt.astype(jnp.bfloat16)
    st = jnp.dot(kn_ref[...], qt, preferred_element_type=jnp.float32)
    c = math.log2(math.e) / math.sqrt(HD)
    m = jnp.max(st, axis=0, keepdims=True)
    e = jnp.exp2((st - m) * c)
    total = jnp.sum(e, axis=0, keepdims=True)
    out_t = jnp.dot(vt_ref[...], e.astype(jnp.bfloat16), preferred_element_type=jnp.float32)
    out = (out_t / total).T.astype(jnp.bfloat16)
    o_ref[...] = out.reshape(o_ref.shape)


def attend(got, share, span_blocks, gain_q, gain_k):
    src, _, rows, _ = got.shape
    tokens = src * rows
    qb = max(1, min(span_blocks, (4 << 20) // (tokens * rows)))
    steps = span_blocks // qb
    tokens = src * rows
    return pl.pallas_call(
        _attn_kernel,
        out_shape=jax.ShapeDtypeStruct((span_blocks, rows, HD), jnp.bfloat16),
        grid_spec=pltpu.PrefetchScalarGridSpec(
            num_scalar_prefetch=1,
            grid=(steps,),
            in_specs=[
                pl.BlockSpec((qb, None, rows, HD), lambda i, sh: (sh[0] * steps + i, 0, 0, 0)),
                pl.BlockSpec((src, None, rows, HD), lambda i, sh: (0, 1, 0, 0)),
                pl.BlockSpec((src, None, rows, HD), lambda i, sh: (0, 2, 0, 0)),
                pl.BlockSpec((1, HD), lambda i, sh: (0, 0)),
                pl.BlockSpec((1, HD), lambda i, sh: (0, 0)),
            ],
            out_specs=pl.BlockSpec((qb, rows, HD), lambda i, sh: (i, 0, 0)),
            scratch_shapes=[pltpu.VMEM((tokens, HD), jnp.bfloat16), pltpu.VMEM((HD, tokens), jnp.bfloat16)],
        ),
        compiler_params=pltpu.CompilerParams(
            dimension_semantics=("arbitrary",), vmem_limit_bytes=48 * 1024 * 1024
        ),
    )(share, got, got, got, gain_q.reshape(1, HD), gain_k.reshape(1, HD))


def _pack_kernel(q_ref, k_ref, v_ref, o_ref):
    group = q_ref.shape[1] // HD
    copies = o_ref.shape[0] // group
    for i in range(group):
        for c in range(copies):
            for j, ref in enumerate((q_ref, k_ref, v_ref)):
                o_ref[i * copies + c, j] = ref[:, i * HD:(i + 1) * HD]


def pack(queries, keys, values, copies):
    rows = queries.shape[0]
    group = 8
    spec = pl.BlockSpec((rows, group * HD), lambda g: (0, g))
    return pl.pallas_call(
        _pack_kernel,
        out_shape=jax.ShapeDtypeStruct((HEADS * copies, 3, rows, HD), jnp.bfloat16),
        grid=(HEADS // group,),
        in_specs=[spec, spec, spec],
        out_specs=pl.BlockSpec((group * copies, 3, rows, HD), lambda g: (g, 0, 0, 0)),
    )(queries, keys, values)


def body(queries, keys, values, gain_q, gain_k, w_latent, w_temporal, w_decode):
    devices = lax.axis_size("seq")
    copies = devices // HEADS
    rows = queries.shape[0]

    stacked = pack(queries, keys, values, copies)
    got = lax.all_to_all(stacked, "seq", split_axis=0, concat_axis=0, tiled=True)
    share = lax.axis_index("seq") % copies
    span_blocks = devices // copies
    out = attend(got, jnp.reshape(share, (1,)).astype(jnp.int32), span_blocks, gain_q, gain_k)
    if copies > 1:
        placed = jnp.zeros((copies, span_blocks, rows, HD), jnp.bfloat16)
        placed = lax.dynamic_update_index_in_dim(placed, out, share, 0)
        out = placed.reshape(devices, rows, HD)
    back = lax.all_to_all(out, "seq", split_axis=0, concat_axis=0, tiled=True)
    if copies > 1:
        back = jnp.sum(back.reshape(HEADS, copies, rows, HD).astype(jnp.float32), axis=1)
        back = back.astype(jnp.bfloat16)
    back = back.reshape(HEADS, rows, HD)
    latent = jnp.einsum(
        "hrd,hdc->rc", back, w_latent.reshape(HEADS, HD, -1), preferred_element_type=jnp.float32
    ).astype(jnp.bfloat16)
    attention = jnp.concatenate([back[h] for h in range(HEADS)], axis=1)
    earlier_one = passed_along(latent, "seq", 1)
    earlier_two = passed_along(latent, "seq", 2)
    state = jnp.dot(latent, w_temporal[0], preferred_element_type=jnp.float32)
    state = state + jnp.dot(earlier_one, w_temporal[1], preferred_element_type=jnp.float32)
    state = state + jnp.dot(earlier_two, w_temporal[2], preferred_element_type=jnp.float32)
    act = lax.optimization_barrier(jax.nn.silu(state).astype(jnp.bfloat16))
    decoded = jnp.dot(act, w_decode, preferred_element_type=jnp.float32).astype(jnp.bfloat16)
    return (attention, decoded)


def solution(mesh):
    in_specs = (
        P(("groups", "seq"), None),
        P(("groups", "seq"), None),
        P(("groups", "seq"), None),
        P(),
        P(),
        P(),
        P(),
        P(),
    )
    out_specs = (P(("groups", "seq"), None), P(("groups", "seq"), None))
    return jax.shard_map(body, mesh=mesh, in_specs=in_specs, out_specs=out_specs, check_vma=False)
```
